32 devices in a mesh: dp: 4 (over z), seq: 8 (over y, x, core).
Axes of the slice: x: 2, y: 2, z: 4, core: 2. Of those that a mesh axis runs over, the one named last changes fastest.
Arguments:
- streams: bfloat16 [4, 1024, 4, 2048], P('dp', 'seq'), may hold values from -6 to 6
- segments: int32 [4, 1024], P('dp', 'seq'), may hold values from 0 to 3, as said below
- positions: int32 [4, 1024], P('dp', 'seq'), may hold values from 0 to 1023, as said below
- att_proj: bfloat16 [2048, 6144], P(('dp', 'seq')), may hold values from -0.125 to 0.125
- attn_out: bfloat16 [2048, 2048], P(('dp', 'seq')), may hold values from -1 to 1
- ff_proj: bfloat16 [2048, 16384], P(('dp', 'seq')), may hold values from -0.125 to 0.125
- ff_out: bfloat16 [8192, 2048], P(('dp', 'seq')), may hold values from -0.0625 to 0.0625
- mix_in: float32 [2, 4], replicated, may hold values from 0.25 to 0.75
- mix_res: float32 [2, 4, 4], replicated, may hold values from -0.45 to 1.45
- depth: float32 [2, 4], replicated, may hold values from 0.5 to 1.5
- cotangent: bfloat16 [4, 1024, 4, 2048], P('dp', 'seq'), may hold values from -6 to 6
Outputs:
- streams_out: bfloat16 [4, 1024, 4, 2048], P('dp', 'seq')
- grad_streams: float32 [4, 1024, 4, 2048], P('dp', 'seq')
- grad_att_proj: float32 [2048, 6144], P(('dp', 'seq'))
- grad_attn_out: float32 [2048, 2048], P(('dp', 'seq'))
- grad_ff_proj: float32 [2048, 16384], P(('dp', 'seq'))
- grad_ff_out: float32 [8192, 2048], P(('dp', 'seq'))
- grad_mix_in: float32 [2, 4], replicated
- grad_mix_res: float32 [2, 4, 4], replicated
- grad_depth: float32 [2, 4], replicated
The draws below stay inside these ranges and needn't reach their ends.
Inputs may be any that keep to these rules, and one draw needn't show every extreme that they name: `segments`: 0 marks text; each sequence holds 3 picture pieces numbered 1 to 3, each 256 consecutive tokens; the last token of each sequence is text. `positions`: a text token's position is its index in its sequence; every token of a picture piece has the index of the piece's first token; the last token of each sequence is text.
All inputs are finite; a program needn't handle non-finite values.
Results may differ from the reference program's by a relative error of at most 0.035.
Values may be sent and summed in bfloat16 or wider, within the bound.
A program may use at most 512 MiB of HBM per device.

```python
import jax
import jax.numpy as jnp
from jax import lax

D = 2048
HEADS = 16
HEAD_DIM = 128
FF = 8192
NS = 4
PIECE = 256
PICS = 3
NSEQ = 4
LEN = 1024


def picture_layout(key):
    seq_keys = jax.random.split(jax.random.fold_in(key, 11), NSEQ)

    def single(seq_key):
        cut_points = jnp.sort(jax.random.randint(seq_key, (PICS,), 0, LEN - PICS * PIECE))
        starts = cut_points + jnp.arange(PICS, dtype=jnp.int32) * PIECE
        token_index = jnp.arange(LEN, dtype=jnp.int32)
        inside = (token_index[None, :] >= starts[:, None]) & (token_index[None, :] < starts[:, None] + PIECE)
        numbers = jnp.sum(jnp.where(inside, jnp.arange(1, PICS + 1, dtype=jnp.int32)[:, None], 0), axis=0)
        offset = jnp.sum(jnp.where(inside, token_index[None, :] - starts[:, None], 0), axis=0)
        return (numbers, token_index - offset)
    return jax.vmap(single)(seq_keys)


def draw_segments(key, part):
    return picture_layout(key)[0]


def draw_positions(key, part):
    return picture_layout(key)[1]


def draw_mix_res(key, part):
    jitter = jax.random.uniform(key, (2, NS, NS), jnp.float32, -0.3, 0.3)
    return jnp.eye(NS, dtype=jnp.float32)[None] + jitter


def block_scale(key, shape, cuts, least, high):
    def one(axis_at, blocks):
        heights = jax.random.uniform(jax.random.fold_in(jax.random.fold_in(key, 6), axis_at), (blocks,), jnp.float32, least / len(cuts), high / len(cuts))
        return jnp.repeat(jnp.exp(heights), shape[axis_at] // blocks).reshape((-1,) + (1,) * (len(shape) - axis_at - 1))

    level = one(*cuts[0])
    for cut in cuts[1:]:
        level = level * one(*cut)
    return level


def normal_values(rng, extent, spread, bound, cuts=(), held_as=jnp.bfloat16):
    values = spread * jax.random.normal(rng, extent, jnp.float32)
    if cuts:
        values = values * block_scale(rng, extent, cuts, -0.22, 0.18)
    return jnp.clip(values, -bound, bound).astype(held_as)


def setup_inputs(seed: int = 0) -> dict:
    seeds = jax.random.split(jax.random.key(seed), 12)
    return {
        "streams": normal_values(seeds[0], (NSEQ, LEN, NS, D), 1.0, 6.0, ((0, 4), (1, 8))),
        "segments": draw_segments(jax.random.fold_in(seeds[11], 71), 0),
        "positions": draw_positions(jax.random.fold_in(seeds[11], 71), 0),
        "att_proj": normal_values(seeds[3], (D, 3 * D), D ** -0.5, 0.125, ((0, 32),)),
        "attn_out": normal_values(seeds[4], (D, D), (D // 64) ** -0.5, 1.0, ((0, 32),)),
        "ff_proj": normal_values(seeds[5], (D, 2 * FF), D ** -0.5, 0.125, ((0, 32),)),
        "ff_out": normal_values(seeds[6], (FF, D), FF ** -0.5, 0.0625, ((0, 32),)),
        "mix_in": jnp.clip(jax.random.uniform(seeds[7], (2, NS), jnp.float32, 0.25, 0.75), 0.25, 0.75),
        "mix_res": draw_mix_res(jax.random.fold_in(seeds[11], 71), 0),
        "depth": jnp.clip(jax.random.uniform(seeds[9], (2, NS), jnp.float32, 0.5, 1.5), 0.5, 1.5),
        "cotangent": normal_values(seeds[10], (NSEQ, LEN, NS, D), 1.0, 6.0, ((0, 4), (1, 8))),
    }


ln_eps = 1e-05
rope_base = 10000.0
neg_big = -1e+30
highest = lax.Precision.HIGHEST

@jax.custom_vjp
def low(v):
    return lax.optimization_barrier(v.astype(jnp.bfloat16)).astype(jnp.float32)

@jax.custom_vjp
def low_back(v):
    return v

def low_keep(v):
    return (low(v), None)

def low_pass(kept, grad):
    return (grad,)

def back_keep(v):
    return (v, None)

def back_low(kept, grad):
    return (low(grad),)
low.defvjp(low_keep, low_pass)
low_back.defvjp(back_keep, back_low)

def layer_norm(values):
    row_mean = lax.optimization_barrier(jnp.mean(values, axis=-1, keepdims=True))
    centered = values - row_mean
    row_var = lax.optimization_barrier(jnp.mean(centered * centered, axis=-1, keepdims=True))
    return centered * lax.rsqrt(row_var + ln_eps)

def rope_tables(positions, head_dim):
    half_dim = head_dim // 2
    inv_freq = rope_base ** (-(jnp.arange(half_dim, dtype=jnp.float32) * 2.0 / head_dim))
    angles = positions.astype(jnp.float32)[..., None] * inv_freq
    angles = jnp.concatenate([angles, angles], axis=-1)
    return (jnp.cos(angles), jnp.sin(angles))

def rotate(values, cosine, sine_table):
    half_dim = values.shape[-1] // 2
    turned = jnp.concatenate([-values[..., half_dim:], values[..., :half_dim]], axis=-1)
    return values * cosine + turned * sine_table

def mix_streams(streams_in, weights):
    return lax.optimization_barrier(jnp.sum(streams_in * weights[None, :, None], axis=1))

def cross_streams(streams_in, matrix):
    return jnp.einsum('rid,ij->rjd', streams_in, matrix, precision=highest)

def attend(queries, keys_in, values_in, segments):
    length = queries.shape[0]
    block_rows = min(512, length)
    key_index = jnp.arange(length, dtype=jnp.int32)
    score_scale = HEAD_DIM ** (-0.5)

    def one_block(block_index):
        first_row = block_index * block_rows
        query_rows = lax.dynamic_slice_in_dim(queries, first_row, block_rows, 0)
        seg_rows = lax.dynamic_slice_in_dim(segments, first_row, block_rows, 0)
        row_index = first_row + jnp.arange(block_rows, dtype=jnp.int32)
        raw_scores = jnp.einsum('qhd,khd->hqk', query_rows, keys_in, precision=highest)
        scores = low_back(raw_scores * score_scale)
        allowed = (key_index[None, :] <= row_index[:, None]) | (segments[None, :] == seg_rows[:, None]) & (seg_rows[:, None] > 0)
        scores = jnp.where(allowed[None], scores, neg_big)
        attn_probs = low(jax.nn.softmax(scores, axis=-1))
        return jnp.einsum('hqk,khd->qhd', attn_probs, values_in, precision=highest)
    attended_all = lax.map(jax.checkpoint(one_block), jnp.arange(length // block_rows, dtype=jnp.int32))
    return attended_all.reshape(length, HEADS * HEAD_DIM)

def hyper_layer(streams_in, segments, positions, att_proj, attn_out, ff_proj, ff_out, mix_in, mix_res, depth):
    length = streams_in.shape[0]
    mixed = mix_streams(streams_in, mix_in[0])
    normed = low(layer_norm(mixed))
    projected = low_back(jnp.dot(normed, att_proj, precision=highest))
    pieces = projected.reshape(length, 3, HEADS, HEAD_DIM)
    cosine, sine_table = rope_tables(positions, HEAD_DIM)
    cosine = cosine[:, None, :]
    sine_table = sine_table[:, None, :]
    queries = low(rotate(pieces[:, 0], cosine, sine_table))
    keys_rot = low(rotate(pieces[:, 1], cosine, sine_table))
    values_in = low(pieces[:, 2])
    attended = low(low_back(attend(queries, keys_rot, values_in, segments)))
    branch = low_back(jnp.dot(attended, attn_out, precision=highest))
    streams_mid = cross_streams(streams_in, mix_res[0]) + depth[0][None, :, None] * branch[:, None, :]
    mixed = mix_streams(streams_mid, mix_in[1])
    normed = low(layer_norm(mixed))
    upgate = low_back(jnp.dot(normed, ff_proj, precision=highest))
    hidden = low(jax.nn.silu(upgate[:, FF:]) * upgate[:, :FF])
    branch = low_back(jnp.dot(hidden, ff_out, precision=highest))
    return cross_streams(streams_mid, mix_res[1]) + depth[1][None, :, None] * branch[:, None, :]

def reference(streams, segments, positions, att_proj, attn_out, ff_proj, ff_out, mix_in, mix_res, depth, cotangent):
    weights = (att_proj.astype(jnp.float32), attn_out.astype(jnp.float32), ff_proj.astype(jnp.float32), ff_out.astype(jnp.float32), mix_in, mix_res, depth)

    def one_sequence(totals, inputs):
        seq_streams, seq_segments, seq_positions, seq_cotangent = inputs

        def apply_layer(streams_in, wa, wb, wc, wd, we, wf, wg):
            return hyper_layer(streams_in, seq_segments, seq_positions, wa, wb, wc, wd, we, wf, wg)
        result, pullback = jax.vjp(apply_layer, seq_streams.astype(jnp.float32), *weights)
        gradients = pullback(seq_cotangent.astype(jnp.float32))
        totals = tuple((total + grad for total, grad in zip(totals, gradients[1:])))
        return (totals, (result.astype(jnp.bfloat16), gradients[0]))
    initial = tuple((jnp.zeros_like(weight) for weight in weights))
    totals, (outputs, grad_streams) = lax.scan(one_sequence, initial, (streams, segments, positions, cotangent))
    return (outputs, grad_streams, totals[0], totals[1], totals[2], totals[3], totals[4], totals[5], totals[6])
```

```python
import jax
import jax.numpy as jnp
from jax import lax
from jax.sharding import PartitionSpec as P

HEADS = 16
HEAD_DIM = 128

ln_eps = 1e-05
rope_base = 10000.0
neg_big = -1e30
f32 = jnp.float32
bf16 = jnp.bfloat16


def dot(a, b, dims):
    return lax.dot_general(a, b, (dims, ((), ())), preferred_element_type=f32)


def norm_stats(values):
    mean = jnp.mean(values, axis=-1, keepdims=True)
    centered = values - mean
    inv = lax.rsqrt(jnp.mean(centered * centered, axis=-1, keepdims=True) + ln_eps)
    return centered * inv, inv


def norm_back(grad, unit, inv):
    mean = jnp.mean(grad, axis=-1, keepdims=True)
    proj = jnp.mean(grad * unit, axis=-1, keepdims=True)
    return (grad - mean - unit * proj) * inv


def rope_tables(positions):
    half = HEAD_DIM // 2
    inv_freq = rope_base ** (-(jnp.arange(half, dtype=f32) * 2.0 / HEAD_DIM))
    angles = positions.astype(f32)[..., None] * inv_freq
    angles = jnp.concatenate([angles, angles], axis=-1)
    return jnp.cos(angles), jnp.sin(angles)


def turn(values):
    half = HEAD_DIM // 2
    return jnp.concatenate([-values[..., half:], values[..., :half]], axis=-1)


def turn_back(values):
    half = HEAD_DIM // 2
    return jnp.concatenate([values[..., half:], -values[..., :half]], axis=-1)


def body(n_dp, n_seq, streams, segments, positions, att_proj, attn_out, ff_proj, ff_out,
         mix_in, mix_res, depth, cotangent):
    seq_count, toks, n_str, width = streams.shape
    assert seq_count == 1
    n_all = n_dp * n_seq
    both = ("dp", "seq")
    rows = att_proj.shape[0]
    ffl = ff_out.shape[0]
    hp = HEADS // n_seq
    hw = hp * HEAD_DIM
    length = toks * n_seq
    scale = HEAD_DIM ** -0.5
    seq_id = lax.axis_index("seq")

    def mix(parts, weights):
        total = parts[0] * weights[0]
        for i in range(1, n_str):
            total = total + parts[i] * weights[i]
        return total

    wq = att_proj.reshape(rows, 3, n_seq, hw)
    wq = lax.all_to_all(wq, "seq", 2, 0, tiled=True).reshape(n_seq * rows, 3 * hw)
    wq = lax.all_gather(wq, "dp", axis=0, tiled=True)
    wf = ff_proj.reshape(rows, 2, n_all, ffl)
    wf = lax.all_to_all(wf, both, 2, 0, tiled=True).reshape(n_all * rows, 2 * ffl)
    wo = lax.all_gather(attn_out, both, axis=0, tiled=True)
    wo = lax.dynamic_slice_in_dim(wo, seq_id * hw, hw, 0)
    seg_all = lax.all_gather(segments[0], "seq", axis=0, tiled=True)
    pos_all = lax.all_gather(positions[0], "seq", axis=0, tiled=True)

    s_in = [streams[0, :, i].astype(f32) for i in range(n_str)]
    cot = [cotangent[0, :, i].astype(f32) for i in range(n_str)]
    d_branch_ff = mix(cot, depth[1]).astype(bf16)
    dbf = lax.all_gather(d_branch_ff, both, axis=0, tiled=True)

    unit_att, inv_att = norm_stats(mix(s_in, mix_in[0]))
    xa = lax.all_gather(unit_att.astype(bf16), "seq", axis=0, tiled=True)
    proj = dot(xa, wq, ((1,), (0,))).reshape(length, 3, hp, HEAD_DIM)
    cosine, sine = rope_tables(pos_all)
    cosine, sine = cosine[:, None], sine[:, None]
    q = (proj[:, 0] * cosine + turn(proj[:, 0]) * sine).astype(bf16)
    k = (proj[:, 1] * cosine + turn(proj[:, 1]) * sine).astype(bf16)
    v = proj[:, 2].astype(bf16)
    idx = jnp.arange(length, dtype=jnp.int32)
    allowed = (idx[None, :] <= idx[:, None]) | (
        (seg_all[None, :] == seg_all[:, None]) & (seg_all[:, None] > 0))
    scores = jnp.einsum("qhd,khd->hqk", q, k, preferred_element_type=f32) * scale
    scores = jnp.where(allowed[None], scores, neg_big)
    top = jnp.max(scores, axis=-1, keepdims=True)
    p = jnp.exp(scores - top)
    p = p / jnp.sum(p, axis=-1, keepdims=True)
    p_low = p.astype(bf16)
    att = jnp.einsum("hqk,khd->qhd", p_low, v, preferred_element_type=f32)
    att = att.reshape(length, hw).astype(bf16)
    branch_att = lax.psum_scatter(dot(att, wo, ((1,), (0,))).astype(bf16), "seq",
                                  scatter_dimension=0, tiled=True).astype(f32)

    mid = [mix(s_in, mix_res[0, :, j]) + depth[0, j] * branch_att for j in range(n_str)]
    unit_ff, inv_ff = norm_stats(mix(mid, mix_in[1]))
    xf = lax.all_gather(unit_ff.astype(bf16), both, axis=0, tiled=True)
    upgate = dot(xf, wf, ((1,), (0,)))
    up, gate = upgate[:, :ffl], upgate[:, ffl:]
    sig = 1.0 / (1.0 + jnp.exp(-gate))
    hidden = (gate * sig * up).astype(bf16)
    branch_ff = lax.psum_scatter(dot(hidden, ff_out, ((1,), (0,))).astype(bf16), both,
                                 scatter_dimension=0, tiled=True).astype(f32)

    d_hidden = dot(dbf, ff_out, ((1,), (1,)))
    g_ff_out = dot(hidden, dbf, ((0,), (0,)))
    d_up = d_hidden * gate * sig
    d_gate = d_hidden * up * (sig * (1.0 + gate * (1.0 - sig)))
    d_ug = jnp.concatenate([d_up, d_gate], axis=1).astype(bf16)
    d_unit = lax.psum_scatter(dot(d_ug, wf, ((1,), (1,))).astype(bf16), both,
                              scatter_dimension=0, tiled=True).astype(f32)
    g_wf = dot(xf, d_ug, ((0,), (0,))).astype(bf16).reshape(n_all, rows, 2 * ffl)
    g_wf = lax.all_to_all(g_wf, both, 0, 0, tiled=True)
    g_ff_proj = g_wf.reshape(n_all, rows, 2, ffl).transpose(1, 2, 0, 3).reshape(ff_proj.shape).astype(f32)
    d_mix_ff = norm_back(d_unit, unit_ff, inv_ff)

    d_mid = [mix(cot, mix_res[1, i]) + mix_in[1, i] * d_mix_ff for i in range(n_str)]
    d_branch_att = mix(d_mid, depth[0]).astype(bf16)
    dba = lax.all_gather(d_branch_att, "seq", axis=0, tiled=True)
    d_att = dot(dba, wo, ((1,), (1,))).astype(bf16).reshape(length, hp, HEAD_DIM)
    g_wo = dot(att, dba, ((0,), (0,))).astype(bf16)
    g_wo = lax.all_gather(g_wo, "seq", axis=0, tiled=True)
    g_attn_out = lax.psum_scatter(g_wo, "dp", scatter_dimension=0, tiled=True)
    g_attn_out = lax.dynamic_slice_in_dim(g_attn_out, seq_id * rows, rows, 0).astype(f32)

    d_v = jnp.einsum("hqk,qhd->khd", p_low, d_att, preferred_element_type=f32)
    d_p = jnp.einsum("qhd,khd->hqk", d_att, v, preferred_element_type=f32)
    d_s = (p * (d_p - jnp.sum(p * d_p, axis=-1, keepdims=True))).astype(bf16)
    d_q = jnp.einsum("hqk,khd->qhd", d_s, k, preferred_element_type=f32) * scale
    d_k = jnp.einsum("hqk,qhd->khd", d_s, q, preferred_element_type=f32) * scale
    d_q = d_q * cosine + turn_back(d_q * sine)
    d_k = d_k * cosine + turn_back(d_k * sine)
    d_proj = jnp.stack([d_q, d_k, d_v], axis=1).reshape(length, 3 * hw).astype(bf16)
    d_unit_att = lax.psum_scatter(dot(d_proj, wq, ((1,), (1,))).astype(bf16), "seq",
                                  scatter_dimension=0, tiled=True).astype(f32)
    g_wq = dot(xa, d_proj, ((0,), (0,))).astype(bf16)
    g_wq = lax.psum_scatter(g_wq, "dp", scatter_dimension=0, tiled=True)
    g_wq = lax.all_to_all(g_wq.reshape(n_seq, rows, 3 * hw), "seq", 0, 0, tiled=True)
    g_att_proj = g_wq.reshape(n_seq, rows, 3, hw).transpose(1, 2, 0, 3).reshape(att_proj.shape).astype(f32)
    d_mix_att = norm_back(d_unit_att, unit_att, inv_att)

    g_in = [mix(d_mid, mix_res[0, i]) + mix_in[0, i] * d_mix_att for i in range(n_str)]
    out = [mix(mid, mix_res[1, :, j]) + depth[1, j] * branch_ff for j in range(n_str)]

    def inner(a, b):
        return jnp.sum(a * b)

    g_mix_in = jnp.stack([
        jnp.stack([inner(s, d_mix_att) for s in s_in]),
        jnp.stack([inner(m, d_mix_ff) for m in mid])])
    g_mix_res = jnp.stack([
        jnp.stack([jnp.stack([inner(s, d) for d in d_mid]) for s in s_in]),
        jnp.stack([jnp.stack([inner(m, c) for c in cot]) for m in mid])])
    g_depth = jnp.stack([
        jnp.stack([inner(branch_att, d) for d in d_mid]),
        jnp.stack([inner(branch_ff, c) for c in cot])])
    g_mix_in, g_mix_res, g_depth = lax.psum((g_mix_in, g_mix_res, g_depth), both)
    return (jnp.stack(out, axis=1).astype(bf16)[None], jnp.stack(g_in, axis=1)[None],
            g_att_proj, g_attn_out, g_ff_proj, g_ff_out, g_mix_in, g_mix_res, g_depth)


def solution(mesh):
    n_dp, n_seq = mesh.shape["dp"], mesh.shape["seq"]
    tok = P("dp", "seq", None, None)
    ids = P("dp", "seq")
    mat = P(("dp", "seq"), None)

    def run(*args):
        return body(n_dp, n_seq, *args)

    return jax.shard_map(
        run, mesh=mesh,
        in_specs=(tok, ids, ids, mat, mat, mat, mat, P(), P(), P(), tok),
        out_specs=(tok, tok, mat, mat, mat, mat, P(), P(), P()),
        check_vma=False)
```

```python
import functools

import jax
import jax.numpy as jnp
from jax import lax
from jax.experimental import pallas as pl
from jax.experimental.pallas import tpu as pltpu
from jax.sharding import PartitionSpec as P

HEADS = 16
HEAD_DIM = 128

ln_eps = 1e-05
rope_base = 10000.0
neg_big = -1e30
f32 = jnp.float32
bf16 = jnp.bfloat16


MESH = pl.DeviceIdType.MESH
DMA = pltpu.SemaphoreType.DMA
ANY = pl.BlockSpec(memory_space=pl.ANY)
VM = pl.BlockSpec(memory_space=pltpu.VMEM)

def greet(peers):
    bar = pltpu.get_barrier_semaphore()
    for p in peers:
        pl.semaphore_signal(bar, inc=1, device_id=p, device_id_type=MESH)
    pl.semaphore_wait(bar, len(peers))

def remote(src, dst, ss, rs, dev):
    return pltpu.make_async_remote_copy(src_ref=src, dst_ref=dst, send_sem=ss, recv_sem=rs, device_id=dev, device_id_type=MESH)

def place():
    z = lax.axis_index("dp"); s = lax.axis_index("seq")
    c = s // 2; k = lax.rem(s, 2)
    xc = c + 1 - 2 * lax.rem(c, 2)
    yc = lax.rem(c + 2, 4)
    dc = lax.rem(xc + 2, 4)
    return z, s, c, k, xc, yc, dc

def add_rows(dst, srcs, first, count, step=16):
    def one(i, _):
        rows = pl.ds(pl.multiple_of(first + i * step, step), step)
        total = srcs[0][rows, :].astype(f32)
        for src in srcs[1:]:
            total = total + src[rows, :].astype(f32)
        dst[rows, :] = total.astype(dst.dtype)
        return 0
    lax.fori_loop(0, count // step, one, 0)

def rs_kernel(nz, trans, a, b, out, pp, po, ra, rd, fx, fy, fz, p_s, p_r, d_s, d_r, x_s, x_r, y_s, y_r, z_s, z_r):
    z, s, c, k, xc, yc, dc = place()
    rows = out.shape[0]; half = rows // 2
    partner = (z, s + 1 - 2 * k)
    dev_x = (z, 2 * xc + k); dev_y = (z, 2 * yc + k)
    zt = [lax.rem(z + i, nz) for i in range(1, nz)]
    greet([partner, dev_x, dev_y] + [(t, s) for t in zt])
    dims = (((1,), (1,)), ((), ())) if trans else (((1,), (0,)), ((), ()))
    cx = lax.rem(c, 2); cy = c // 2
    def produce(i, _):
        j = lax.rem(i, 4)
        rx = jnp.where(j < 2, 1, 0); ry = jnp.where(lax.rem(j, 2) == 0, 1, 0) * jnp.where(j < 3, 1, 0)
        px = cx + rx - 2 * cx * rx; py = cy + ry - 2 * cy * ry
        blk = px + 2 * py
        if nz > 1:
            blk = blk + lax.rem(z + 1 + i // 4, nz) * 4
        at = pl.ds(pl.multiple_of(blk * 2 * rows, 2 * rows), 2 * rows)
        both = lax.dot_general(a[at, :], b[...], dims, preferred_element_type=f32).astype(bf16)
        pp[i, 0] = both[:rows]
        pp[i, 1] = both[rows:]
        remote(pp.at[i, 1 - k], ra.at[i], p_s.at[i], p_r.at[i], partner).start()
        return 0
    lo, hi = pl.ds(0, half), pl.ds(half, half)
    def first(zi):
        for j in range(4):
            q = zi * 4 + j
            remote(ra.at[q], ra.at[q], p_s.at[q], p_r.at[q], partner).wait_recv()
            add_rows(po.at[q], [pp.at[q, k], ra.at[q]], 0, rows)
            if j == 0:
                remote(po.at[q, lo], rd.at[zi, lo], d_s.at[zi, 0], d_r.at[zi, 0], dev_x).start()
                remote(po.at[q, hi], rd.at[zi, hi], d_s.at[zi, 1], d_r.at[zi, 1], dev_y).start()
            if j == 1:
                remote(po.at[q, lo], fx.at[zi, lo], x_s.at[zi, 0], x_r.at[zi, 0], dev_x).start()
            if j == 2:
                remote(po.at[q, hi], fy.at[zi, hi], y_s.at[zi, 1], y_r.at[zi, 1], dev_y).start()
    def second(zi):
        qx, qy = zi * 4 + 1, zi * 4 + 2
        remote(rd.at[zi, lo], rd.at[zi, lo], d_s.at[zi, 0], d_r.at[zi, 0], dev_x).wait_recv()
        add_rows(po.at[qy], [po.at[qy], rd.at[zi]], 0, half)
        remote(po.at[qy, lo], fy.at[zi, lo], y_s.at[zi, 0], y_r.at[zi, 0], dev_y).start()
        remote(rd.at[zi, hi], rd.at[zi, hi], d_s.at[zi, 1], d_r.at[zi, 1], dev_y).wait_recv()
        add_rows(po.at[qx], [po.at[qx], rd.at[zi]], half, half)
        remote(po.at[qx, hi], fx.at[zi, hi], x_s.at[zi, 1], x_r.at[zi, 1], dev_x).start()
    def third(zi):
        q = zi * 4 + 3
        for h, part in ((0, lo), (1, hi)):
            remote(fx.at[zi, part], fx.at[zi, part], x_s.at[zi, h], x_r.at[zi, h], dev_x).wait_recv()
            remote(fy.at[zi, part], fy.at[zi, part], y_s.at[zi, h], y_r.at[zi, h], dev_y).wait_recv()
        if zi < nz - 1:
            add_rows(po.at[q], [po.at[q], fx.at[zi], fy.at[zi]], 0, rows)
            remote(po.at[q], fz.at[zi], z_s.at[zi], z_r.at[zi], (zt[zi], s)).start()
        else:
            for i in range(nz - 1):
                remote(fz.at[i], fz.at[i], z_s.at[i], z_r.at[i], (zt[i], s)).wait_recv()
            add_rows(out, [po.at[q], fx.at[zi], fy.at[zi]] + [fz.at[i] for i in range(nz - 1)], 0, rows)
    lax.fori_loop(0, 4, produce, 0)
    for t in range(nz + 2):
        if t + 1 < nz: lax.fori_loop(4 * t + 4, 4 * t + 8, produce, 0)
        if t < nz: first(t)
        if 0 <= t - 1 < nz: second(t - 1)
        if 0 <= t - 2 < nz: third(t - 2)
    for q in range(4 * nz):
        remote(ra.at[q], ra.at[q], p_s.at[q], p_r.at[q], partner).wait_send()
    for zi in range(nz):
        for h, part in ((0, lo), (1, hi)):
            remote(rd.at[zi, part], rd.at[zi, part], d_s.at[zi, h], d_r.at[zi, h], dev_x).wait_send()
            remote(fx.at[zi, part], fx.at[zi, part], x_s.at[zi, h], x_r.at[zi, h], dev_x).wait_send()
            remote(fy.at[zi, part], fy.at[zi, part], y_s.at[zi, h], y_r.at[zi, h], dev_y).wait_send()
    for i in range(nz - 1):
        remote(fz.at[i], fz.at[i], z_s.at[i], z_r.at[i], (zt[i], s)).wait_send()

def dot_scatter(a, b, nz, trans, cid):
    rows = a.shape[0] // (8 * nz); width = b.shape[0] if trans else b.shape[1]
    m = max(nz - 1, 1)
    blk = lambda n: pltpu.VMEM((n, rows, width), bf16)
    return pl.pallas_call(
        functools.partial(rs_kernel, nz, trans),
        out_shape=jax.ShapeDtypeStruct((rows, width), f32),
        in_specs=[VM, VM], out_specs=VM,
        scratch_shapes=[pltpu.VMEM((4*nz, 2, rows, width), bf16), blk(4*nz), blk(4*nz), blk(nz), blk(nz), blk(nz), blk(m),
                        DMA((4*nz,)), DMA((4*nz,)), DMA((nz,2)), DMA((nz,2)), DMA((nz,2)), DMA((nz,2)), DMA((nz,2)), DMA((nz,2)), DMA((m,)), DMA((m,))],
        compiler_params=pltpu.CompilerParams(collective_id=cid, has_side_effects=True, vmem_limit_bytes=60*1024*1024),
    )(a, b)


class Gather:
    def __init__(self, nz, x, out, sems):
        self.zs, self.zr, self.cs, self.cr, self.ds, self.dr, self.ps, self.pr, self.ls = sems
        self.nz, self.x, self.out = nz, x, out
        self.z, self.s, self.c, self.k, self.xc, self.yc, self.dc = place()
        z, s, k = self.z, self.s, self.k
        self.half = x.shape[0] // 2
        self.zt = [(lax.rem(z + i, nz), s) for i in range(1, nz)]
        self.dev = [(z, 2 * self.xc + k), (z, 2 * self.yc + k)]
        self.partner = (z, s + 1 - 2 * k)
        self.src = [z] + [lax.rem(z + nz - i, nz) for i in range(1, nz)]
        self.sends = []
        self.np = 0
        self.nw = 0

    def peers(self):
        return self.zt + self.dev + [self.partner]

    def at(self, zi, chip, core, part=None):
        idx = (chip, core) if self.nz == 1 else (self.src[zi], chip, core)
        if part is not None:
            idx = idx + (pl.ds(part * self.half, self.half),)
        return self.out.at[idx]

    def go(self, *args):
        d = remote(*args)
        d.start()
        self.sends.append(d)

    def pair(self, src, dst):
        self.go(src, dst, self.ps.at[self.np], self.pr.at[self.np], self.partner)
        self.np += 1

    def plane(self, zi, src, dst):
        for j in range(2):
            self.go(src, dst, self.cs.at[zi, j], self.cr.at[zi, j], self.dev[j])

    def begin(self):
        own = self.at(0, self.c, self.k)
        self.local = pltpu.make_async_copy(self.x, own, self.ls)
        self.local.start()
        self.plane(0, self.x, own)
        for i in range(1, self.nz):
            self.go(self.x, own, self.zs.at[i - 1], self.zr.at[i - 1], self.zt[i - 1])
        self.pair(self.x, own)

    def line(self, zi):
        blk = self.at(zi, self.c, self.k)
        remote(blk, blk, self.zs.at[zi - 1], self.zr.at[zi - 1], self.zt[zi - 1]).wait_recv()
        self.plane(zi, blk, blk)
        self.pair(blk, blk)

    def near(self, zi, j):
        chip = (self.xc, self.yc)[j]
        blk = self.at(zi, chip, self.k)
        remote(blk, blk, self.cs.at[zi, j], self.cr.at[zi, j], self.dev[j]).wait_recv()
        part = self.at(zi, chip, self.k, j)
        self.go(part, part, self.ds.at[zi, j], self.dr.at[zi, j], self.dev[1 - j])
        self.pair(blk, blk)

    def far(self, zi, h):
        part = self.at(zi, self.dc, self.k, h)
        remote(part, part, self.ds.at[zi, h], self.dr.at[zi, h], self.dev[1 - h]).wait_recv()
        self.pair(part, part)

    def wait_pair(self, blk):
        remote(blk, blk, self.ps.at[self.nw], self.pr.at[self.nw], self.partner).wait_recv()
        self.nw += 1

    def steps(self):
        nz = self.nz
        other = 1 - self.k
        todo = []
        for t in range(nz + 2):
            if 1 <= t < nz:
                todo.append((lambda t=t: self.line(t), lambda t=t: self.at(t, self.c, other)))
            u = t - 1 if nz > 1 else t
            if 0 <= u < nz:
                for j in range(2):
                    todo.append((lambda u=u, j=j: self.near(u, j), lambda u=u, j=j: self.at(u, (self.xc, self.yc)[j], other)))
            u = u - 1
            if 0 <= u < nz:
                for h in range(2):
                    todo.append((lambda u=u, h=h: self.far(u, h), lambda u=u, h=h: self.at(u, self.dc, other, h)))
        return todo

    def finish(self, todo):
        self.wait_pair(self.at(0, self.c, 1 - self.k))
        for _, blk in todo:
            self.wait_pair(blk())
        for d in self.sends:
            d.wait_send()
        self.local.wait()


def gather_sems(nz):
    m = max(nz - 1, 1)
    return [DMA((m,)), DMA((m,)), DMA((nz, 2)), DMA((nz, 2)), DMA((nz, 2)), DMA((nz, 2)),
            DMA((nz * 5,)), DMA((nz * 5,)), DMA]


def gather_kernel(nz, x, out, *sems):
    g = Gather(nz, x, out, sems)
    greet(g.peers())
    g.begin()
    todo = g.steps()
    for act, _ in todo:
        act()
    g.finish(todo)


def all_gather(x, nz, cid):
    rows, width = x.shape
    shape = (4, 2, rows, width) if nz == 1 else (nz, 4, 2, rows, width)
    out = pl.pallas_call(
        functools.partial(gather_kernel, nz),
        out_shape=jax.ShapeDtypeStruct(shape, x.dtype), in_specs=[ANY], out_specs=ANY,
        scratch_shapes=gather_sems(nz),
        compiler_params=pltpu.CompilerParams(collective_id=cid, has_side_effects=True))(x)
    return out.reshape(8 * nz * rows, width)


def head_kernel(n_dp, x, ids, wp, wo, xa, ids_all, wq, wo_mine, *sems):
    gs = sems[:9]
    i_s, i_r, q_s, q_r, u_s, u_r, v_s, v_r, o_s, o_r, l_s = sems[9:]
    z, s, c, k, xc, yc, dc = place()
    n_seq = 8
    rows = wp.shape[0]
    w = wp.shape[1] // (3 * n_seq)
    me = z * n_seq + s
    g = Gather(1, x, xa, gs)
    everyone = []
    for i in range(1, n_dp * n_seq):
        t = lax.rem(me + i, n_dp * n_seq)
        everyone.append((t // n_seq, lax.rem(t, n_seq)))
    greet(everyone)
    sends = []
    locals_ = []

    def go(*args):
        d = remote(*args)
        d.start()
        sends.append(d)

    def piece(plane, t):
        return wq.at[pl.ds(pl.multiple_of((plane * n_seq + t) * rows, rows), rows)]

    def cols(t, j):
        return wp.at[:, pl.ds(pl.multiple_of(j * n_seq * w + t * w, w), w)]
    seqs = [lax.rem(s + i, n_seq) for i in range(n_seq)]
    back = [lax.rem(s + n_seq - i, n_seq) for i in range(n_seq)]
    mine = piece(z, s)
    for j in range(3):
        d = pltpu.make_async_copy(cols(s, j), mine.at[:, pl.ds(j * w, w)], l_s.at[j])
        d.start()
        locals_.append(d)
    for i in range(1, n_seq):
        for j in range(3):
            go(cols(seqs[i], j), mine.at[:, pl.ds(j * w, w)], q_s.at[i], q_r.at[i], (z, seqs[i]))
    for i in range(1, n_seq):
        own = ids_all.at[s]
        go(ids, own, i_s.at[i], i_r.at[i], (z, seqs[i]))
    d = pltpu.make_async_copy(ids, ids_all.at[s], l_s.at[3])
    d.start()
    locals_.append(d)
    g.begin()
    up, down = z < n_dp - 1, z > 0
    chain = []

    def send_up(h, plane, t):
        p = piece(plane, t)
        return remote(p, p, u_s.at[h, t], u_r.at[h, t], (z + 1, s))

    def send_down(h, plane, t):
        p = piece(plane, t)
        return remote(p, p, v_s.at[h, t], v_r.at[h, t], (z - 1, s))

    def first(i):
        if i == 0:
            for d in locals_[:3]:
                d.wait()
        else:
            p = piece(z, back[i])
            remote(p, p, q_s.at[i], q_r.at[i], (z, back[i])).wait_recv()
        t = back[i]

        @pl.when(up)
        def _():
            send_up(0, z, t).start()

        @pl.when(down)
        def _():
            send_down(0, z, t).start()

    def hop(h, i):
        t = lax.rem(s + n_seq - i, n_seq)

        @pl.when(z >= h)
        def _():
            send_up(h - 1, z - h, t).wait_recv()

            @pl.when(up)
            def _():
                send_up(h, z - h, t).start()

        @pl.when(z + h < n_dp)
        def _():
            send_down(h - 1, z + h, t).wait_recv()

            @pl.when(down)
            def _():
                send_down(h, z + h, t).start()
    for i in range(n_seq):
        first(i)
    dest = me // 4
    for i in range(n_dp):
        zt = lax.rem(z + i, n_dp)
        part = wo_mine.at[pl.ds(pl.multiple_of(lax.rem(me, 4) * rows, rows), rows)]
        if i == 0:
            @pl.when(dest != s)
            def _():
                remote(wo, part, o_s.at[0], o_r.at[lax.rem(me, 4)], (z, dest)).start()

            @pl.when(dest == s)
            def _():
                pltpu.make_async_copy(wo, part, l_s.at[4]).start()
        else:
            go(wo, part, o_s.at[i], o_r.at[lax.rem(me, 4)], (zt, dest))
    todo = g.steps()
    pending = [lambda h=h, i=i: hop(h, i) for h in range(1, n_dp) for i in range(n_seq)]
    for act, _ in todo:
        act()
        for p in pending[:2]:
            p()
        pending = pending[2:]
    for p in pending:
        p()
    for i in range(1, n_seq):
        own = ids_all.at[back[i]]
        remote(own, own, i_s.at[i], i_r.at[i], (z, back[i])).wait_recv()
    for t in range(4):
        src = s * 4 + t
        part = wo_mine.at[pl.ds(t * rows, rows)]

        @pl.when(src != me)
        def _():
            remote(part, part, o_s.at[0], o_r.at[t], (src // n_seq, lax.rem(src, n_seq))).wait_recv()

        @pl.when(src == me)
        def _():
            pltpu.make_async_copy(wo, part, l_s.at[4]).wait()
    g.finish(todo)
    for d in sends:
        d.wait_send()
    for d in locals_[3:]:
        d.wait()

    @pl.when(dest != s)
    def _():
        remote(wo, wo, o_s.at[0], o_r.at[0], (z, dest)).wait_send()
    for h in range(n_dp - 1):
        for i in range(n_seq):
            @pl.when((z >= h) & up)
            def _():
                send_up(h, z - h, back[i]).wait_send()

            @pl.when((z + h < n_dp) & down)
            def _():
                send_down(h, z + h, back[i]).wait_send()


def head_exchange(x, ids, wp, wo, n_dp, cid):
    rows, width = x.shape
    w = wp.shape[1] // 24
    n = n_dp * 8
    return pl.pallas_call(
        functools.partial(head_kernel, n_dp),
        out_shape=(jax.ShapeDtypeStruct((4, 2, rows, width), x.dtype),
                   jax.ShapeDtypeStruct((8,) + ids.shape, ids.dtype),
                   jax.ShapeDtypeStruct((n * wp.shape[0], 3 * w), wp.dtype),
                   jax.ShapeDtypeStruct((4 * wo.shape[0], wo.shape[1]), wo.dtype)),
        in_specs=[ANY] * 4, out_specs=(ANY,) * 4,
        scratch_shapes=gather_sems(1) + [DMA((8,)), DMA((8,)), DMA((8,)), DMA((8,)),
                                         DMA((n_dp, 8)), DMA((n_dp, 8)), DMA((n_dp, 8)), DMA((n_dp, 8)),
                                         DMA((n_dp,)), DMA((4,)), DMA((5,))],
        compiler_params=pltpu.CompilerParams(collective_id=cid, has_side_effects=True))(x, ids, wp, wo)


def tail_kernel(n_dp, gq, go_, small, out_q, out_o, out_s, rz, st, rq, ro, rs, z_s, z_r, q_s, q_r, o_s, o_r, m_s, m_r, l_s):
    z, s, c, k, xc, yc, dc = place()
    n_seq = 8
    rows = out_q.shape[0]
    w = out_q.shape[1] // (3 * n_seq)
    me = z * n_seq + s
    n = n_dp * n_seq
    everyone = []
    for i in range(1, n):
        t = lax.rem(me + i, n)
        everyone.append((t // n_seq, lax.rem(t, n_seq)))
    greet(everyone)
    sends = []

    def go(*args):
        d = remote(*args)
        d.start()
        sends.append(d)
    for i in range(1, n):
        go(small, rs.at[i], m_s.at[i], m_r.at[i], everyone[i - 1])
    seqs = [lax.rem(s + i, n_seq) for i in range(n_seq)]
    order = list(range(1, n_seq)) + [0]

    def part(plane, t):
        return pl.ds(pl.multiple_of((plane * n_seq + t) * rows, rows), rows)
    for i in order:
        for h in range(1, n_dp):
            zt = lax.rem(z + h, n_dp)
            go(gq.at[part(zt, seqs[i])], rz.at[h, i], z_s.at[h, i], z_r.at[h, i], (zt, s))
    for t in range(4):
        d = s * 4 + t
        src = go_.at[pl.ds(t * rows, rows)]

        @pl.when(d != me)
        def _():
            remote(src, ro.at[z], o_s.at[t], o_r.at[z], (d // n_seq, lax.rem(d, n_seq))).start()

        @pl.when(d == me)
        def _():
            pltpu.make_async_copy(src, ro.at[z], l_s).start()
    for i in order:
        for h in range(1, n_dp):
            remote(rz.at[h, i], rz.at[h, i], z_s.at[h, i], z_r.at[h, i], (z, s + 1 - 2 * k)).wait_recv()
        own = gq.at[part(z, seqs[i])]
        if i == 0:
            add_rows(rq.at[0], [own] + [rz.at[h, i] for h in range(1, n_dp)], 0, rows)
        else:
            add_rows(st.at[i], [own] + [rz.at[h, i] for h in range(1, n_dp)], 0, rows)
            go(st.at[i], rq.at[i], q_s.at[i], q_r.at[i], (z, seqs[i]))
    total = small[...]
    for i in range(1, n):
        remote(rs.at[i], rs.at[i], m_s.at[i], m_r.at[i], everyone[0]).wait_recv()
        total = total + rs[i]
    out_s[...] = total
    for t in range(n_dp):
        from_s = me // 4

        @pl.when((z != t) | (s != from_s))
        def _():
            remote(ro.at[t], ro.at[t], o_s.at[0], o_r.at[t], (t, from_s)).wait_recv()

        @pl.when((z == t) & (s == from_s))
        def _():
            pltpu.make_async_copy(ro.at[t], ro.at[t], l_s).wait()
    add_rows(out_o, [ro.at[t] for t in range(n_dp)], 0, rows)
    for i in range(n_seq):
        src = lax.rem(s + n_seq - i, n_seq)
        if i:
            remote(rq.at[i], rq.at[i], q_s.at[i], q_r.at[i], (z, src)).wait_recv()
        for j in range(3):
            at = pl.ds(pl.multiple_of(j * n_seq * w + src * w, w), w)
            out_q[:, at] = rq[i, :, j * w:(j + 1) * w].astype(f32)
    for d in sends:
        d.wait_send()
    for t in range(4):
        d = s * 4 + t
        src = go_.at[pl.ds(t * rows, rows)]

        @pl.when(d != me)
        def _():
            remote(src, ro.at[z], o_s.at[t], o_r.at[z], (d // n_seq, lax.rem(d, n_seq))).wait_send()


def tail_exchange(gq, gwo, small, n_dp, cid):
    n = n_dp * 8
    rows, w3 = gq.shape[0] // n, gq.shape[1]
    return pl.pallas_call(
        functools.partial(tail_kernel, n_dp),
        out_shape=(jax.ShapeDtypeStruct((rows, w3 * 8), f32),
                   jax.ShapeDtypeStruct((rows, gwo.shape[1]), f32),
                   jax.ShapeDtypeStruct(small.shape, f32)),
        in_specs=[VM] * 3, out_specs=(VM,) * 3,
        scratch_shapes=[pltpu.VMEM((n_dp, 8, rows, w3), bf16), pltpu.VMEM((8, rows, w3), bf16),
                        pltpu.VMEM((8, rows, w3), bf16), pltpu.VMEM((n_dp, rows, gwo.shape[1]), bf16),
                        pltpu.VMEM((n,) + small.shape, f32),
                        DMA((n_dp, 8)), DMA((n_dp, 8)), DMA((8,)), DMA((8,)), DMA((4,)), DMA((n_dp,)),
                        DMA((n,)), DMA((n,)), DMA],
        compiler_params=pltpu.CompilerParams(collective_id=cid, has_side_effects=True,
                                             vmem_limit_bytes=48 * 1024 * 1024))(gq, gwo, small)


def dot(a, b, dims):
    return lax.dot_general(a, b, (dims, ((), ())), preferred_element_type=f32)


def norm_stats(values):
    mean = jnp.mean(values, axis=-1, keepdims=True)
    centered = values - mean
    inv = lax.rsqrt(jnp.mean(centered * centered, axis=-1, keepdims=True) + ln_eps)
    return centered * inv, inv


def norm_back(grad, unit, inv):
    mean = jnp.mean(grad, axis=-1, keepdims=True)
    proj = jnp.mean(grad * unit, axis=-1, keepdims=True)
    return (grad - mean - unit * proj) * inv


def rope_tables(positions):
    half = HEAD_DIM // 2
    inv_freq = rope_base ** (-(jnp.arange(half, dtype=f32) * 2.0 / HEAD_DIM))
    angles = positions.astype(f32)[..., None] * inv_freq
    angles = jnp.concatenate([angles, angles], axis=-1)
    return jnp.cos(angles), jnp.sin(angles)


def turn(values):
    half = HEAD_DIM // 2
    return jnp.concatenate([-values[..., half:], values[..., :half]], axis=-1)


def turn_back(values):
    half = HEAD_DIM // 2
    return jnp.concatenate([values[..., half:], -values[..., :half]], axis=-1)


def plain_body(n_dp, n_seq, streams, segments, positions, att_proj, attn_out, ff_proj, ff_out,
         mix_in, mix_res, depth, cotangent):
    seq_count, toks, n_str, width = streams.shape
    assert seq_count == 1
    n_all = n_dp * n_seq
    both = ("dp", "seq")
    rows = att_proj.shape[0]
    ffl = ff_out.shape[0]
    hp = HEADS // n_seq
    hw = hp * HEAD_DIM
    length = toks * n_seq
    scale = HEAD_DIM ** -0.5
    seq_id = lax.axis_index("seq")

    def mix(parts, weights):
        total = parts[0] * weights[0]
        for i in range(1, n_str):
            total = total + parts[i] * weights[i]
        return total

    wq = att_proj.reshape(rows, 3, n_seq, hw)
    wq = lax.all_to_all(wq, "seq", 2, 0, tiled=True).reshape(n_seq * rows, 3 * hw)
    wq = lax.all_gather(wq, "dp", axis=0, tiled=True)
    wf = ff_proj.reshape(rows, 2, n_all, ffl)
    wf = lax.all_to_all(wf, both, 2, 0, tiled=True).reshape(n_all * rows, 2 * ffl)
    wo = lax.all_gather(attn_out, both, axis=0, tiled=True)
    wo = lax.dynamic_slice_in_dim(wo, seq_id * hw, hw, 0)
    seg_all = lax.all_gather(segments[0], "seq", axis=0, tiled=True)
    pos_all = lax.all_gather(positions[0], "seq", axis=0, tiled=True)

    s_in = [streams[0, :, i].astype(f32) for i in range(n_str)]
    cot = [cotangent[0, :, i].astype(f32) for i in range(n_str)]
    d_branch_ff = mix(cot, depth[1]).astype(bf16)
    dbf = lax.all_gather(d_branch_ff, both, axis=0, tiled=True)

    unit_att, inv_att = norm_stats(mix(s_in, mix_in[0]))
    xa = lax.all_gather(unit_att.astype(bf16), "seq", axis=0, tiled=True)
    proj = dot(xa, wq, ((1,), (0,))).reshape(length, 3, hp, HEAD_DIM)
    cosine, sine = rope_tables(pos_all)
    cosine, sine = cosine[:, None], sine[:, None]
    q = (proj[:, 0] * cosine + turn(proj[:, 0]) * sine).astype(bf16)
    k = (proj[:, 1] * cosine + turn(proj[:, 1]) * sine).astype(bf16)
    v = proj[:, 2].astype(bf16)
    idx = jnp.arange(length, dtype=jnp.int32)
    allowed = (idx[None, :] <= idx[:, None]) | (
        (seg_all[None, :] == seg_all[:, None]) & (seg_all[:, None] > 0))
    scores = jnp.einsum("qhd,khd->hqk", q, k, preferred_element_type=f32) * scale
    scores = jnp.where(allowed[None], scores, neg_big)
    top = jnp.max(scores, axis=-1, keepdims=True)
    p = jnp.exp(scores - top)
    p = p / jnp.sum(p, axis=-1, keepdims=True)
    p_low = p.astype(bf16)
    att = jnp.einsum("hqk,khd->qhd", p_low, v, preferred_element_type=f32)
    att = att.reshape(length, hw).astype(bf16)
    branch_att = lax.psum_scatter(dot(att, wo, ((1,), (0,))).astype(bf16), "seq",
                                  scatter_dimension=0, tiled=True).astype(f32)

    mid = [mix(s_in, mix_res[0, :, j]) + depth[0, j] * branch_att for j in range(n_str)]
    unit_ff, inv_ff = norm_stats(mix(mid, mix_in[1]))
    xf = lax.all_gather(unit_ff.astype(bf16), both, axis=0, tiled=True)
    upgate = dot(xf, wf, ((1,), (0,)))
    up, gate = upgate[:, :ffl], upgate[:, ffl:]
    sig = 1.0 / (1.0 + jnp.exp(-gate))
    hidden = (gate * sig * up).astype(bf16)
    branch_ff = lax.psum_scatter(dot(hidden, ff_out, ((1,), (0,))).astype(bf16), both,
                                 scatter_dimension=0, tiled=True).astype(f32)

    d_hidden = dot(dbf, ff_out, ((1,), (1,)))
    g_ff_out = dot(hidden, dbf, ((0,), (0,)))
    d_up = d_hidden * gate * sig
    d_gate = d_hidden * up * (sig * (1.0 + gate * (1.0 - sig)))
    d_ug = jnp.concatenate([d_up, d_gate], axis=1).astype(bf16)
    d_unit = lax.psum_scatter(dot(d_ug, wf, ((1,), (1,))).astype(bf16), both,
                              scatter_dimension=0, tiled=True).astype(f32)
    g_wf = dot(xf, d_ug, ((0,), (0,))).astype(bf16).reshape(n_all, rows, 2 * ffl)
    g_wf = lax.all_to_all(g_wf, both, 0, 0, tiled=True)
    g_ff_proj = g_wf.reshape(n_all, rows, 2, ffl).transpose(1, 2, 0, 3).reshape(ff_proj.shape).astype(f32)
    d_mix_ff = norm_back(d_unit, unit_ff, inv_ff)

    d_mid = [mix(cot, mix_res[1, i]) + mix_in[1, i] * d_mix_ff for i in range(n_str)]
    d_branch_att = mix(d_mid, depth[0]).astype(bf16)
    dba = lax.all_gather(d_branch_att, "seq", axis=0, tiled=True)
    d_att = dot(dba, wo, ((1,), (1,))).astype(bf16).reshape(length, hp, HEAD_DIM)
    g_wo = dot(att, dba, ((0,), (0,))).astype(bf16)
    g_wo = lax.all_gather(g_wo, "seq", axis=0, tiled=True)
    g_attn_out = lax.psum_scatter(g_wo, "dp", scatter_dimension=0, tiled=True)
    g_attn_out = lax.dynamic_slice_in_dim(g_attn_out, seq_id * rows, rows, 0).astype(f32)

    d_v = jnp.einsum("hqk,qhd->khd", p_low, d_att, preferred_element_type=f32)
    d_p = jnp.einsum("qhd,khd->hqk", d_att, v, preferred_element_type=f32)
    d_s = (p * (d_p - jnp.sum(p * d_p, axis=-1, keepdims=True))).astype(bf16)
    d_q = jnp.einsum("hqk,khd->qhd", d_s, k, preferred_element_type=f32) * scale
    d_k = jnp.einsum("hqk,qhd->khd", d_s, q, preferred_element_type=f32) * scale
    d_q = d_q * cosine + turn_back(d_q * sine)
    d_k = d_k * cosine + turn_back(d_k * sine)
    d_proj = jnp.stack([d_q, d_k, d_v], axis=1).reshape(length, 3 * hw).astype(bf16)
    d_unit_att = lax.psum_scatter(dot(d_proj, wq, ((1,), (1,))).astype(bf16), "seq",
                                  scatter_dimension=0, tiled=True).astype(f32)
    g_wq = dot(xa, d_proj, ((0,), (0,))).astype(bf16)
    g_wq = lax.psum_scatter(g_wq, "dp", scatter_dimension=0, tiled=True)
    g_wq = lax.all_to_all(g_wq.reshape(n_seq, rows, 3 * hw), "seq", 0, 0, tiled=True)
    g_att_proj = g_wq.reshape(n_seq, rows, 3, hw).transpose(1, 2, 0, 3).reshape(att_proj.shape).astype(f32)
    d_mix_att = norm_back(d_unit_att, unit_att, inv_att)

    g_in = [mix(d_mid, mix_res[0, i]) + mix_in[0, i] * d_mix_att for i in range(n_str)]
    out = [mix(mid, mix_res[1, :, j]) + depth[1, j] * branch_ff for j in range(n_str)]

    def inner(a, b):
        return jnp.sum(a * b)

    g_mix_in = jnp.stack([
        jnp.stack([inner(s, d_mix_att) for s in s_in]),
        jnp.stack([inner(m, d_mix_ff) for m in mid])])
    g_mix_res = jnp.stack([
        jnp.stack([jnp.stack([inner(s, d) for d in d_mid]) for s in s_in]),
        jnp.stack([jnp.stack([inner(m, c) for c in cot]) for m in mid])])
    g_depth = jnp.stack([
        jnp.stack([inner(branch_att, d) for d in d_mid]),
        jnp.stack([inner(branch_ff, c) for c in cot])])
    g_mix_in, g_mix_res, g_depth = lax.psum((g_mix_in, g_mix_res, g_depth), both)
    return (jnp.stack(out, axis=1).astype(bf16)[None], jnp.stack(g_in, axis=1)[None],
            g_att_proj, g_attn_out, g_ff_proj, g_ff_out, g_mix_in, g_mix_res, g_depth)


def fast_body(n_dp, n_seq, streams, segments, positions, att_proj, attn_out, ff_proj, ff_out,
         mix_in, mix_res, depth, cotangent):
    seq_count, toks, n_str, width = streams.shape
    assert seq_count == 1
    n_all = n_dp * n_seq
    both = ("dp", "seq")
    rows = att_proj.shape[0]
    ffl = ff_out.shape[0]
    hp = HEADS // n_seq
    hw = hp * HEAD_DIM
    length = toks * n_seq
    scale = HEAD_DIM ** -0.5
    seq_id = lax.axis_index("seq")

    def mix(parts, weights):
        total = parts[0] * weights[0]
        for i in range(1, n_str):
            total = total + parts[i] * weights[i]
        return total

    wf = ff_proj.reshape(rows, 2, n_all, ffl).transpose(2, 0, 1, 3).reshape(n_all, rows, 2 * ffl)
    wf = lax.all_to_all(wf, both, 0, 0, tiled=True).reshape(n_all * rows, 2 * ffl)
    s_in = [streams[0, :, i].astype(f32) for i in range(n_str)]
    cot = [cotangent[0, :, i].astype(f32) for i in range(n_str)]
    d_branch_ff = mix(cot, depth[1]).astype(bf16)
    dbf = lax.all_gather(d_branch_ff, both, axis=0, tiled=True)

    unit_att, inv_att = norm_stats(mix(s_in, mix_in[0]))
    ids = jnp.concatenate([segments, positions, jnp.zeros((6, toks), jnp.int32)], axis=0)
    xa, ids_all, wq, wo = head_exchange(unit_att.astype(bf16), ids, att_proj, attn_out, n_dp, 0)
    xa = xa.reshape(length, width)
    seg_all = ids_all[:, 0].reshape(length)
    pos_all = ids_all[:, 1].reshape(length)
    proj = dot(xa, wq, ((1,), (0,))).reshape(length, 3, hp, HEAD_DIM)
    cosine, sine = rope_tables(pos_all)
    cosine, sine = cosine[:, None], sine[:, None]
    q = (proj[:, 0] * cosine + turn(proj[:, 0]) * sine).astype(bf16)
    k = (proj[:, 1] * cosine + turn(proj[:, 1]) * sine).astype(bf16)
    v = proj[:, 2].astype(bf16)
    idx = jnp.arange(length, dtype=jnp.int32)
    allowed = (idx[None, :] <= idx[:, None]) | (
        (seg_all[None, :] == seg_all[:, None]) & (seg_all[:, None] > 0))
    scores = jnp.einsum("qhd,khd->hqk", q, k, preferred_element_type=f32) * scale
    scores = jnp.where(allowed[None], scores, neg_big)
    top = jnp.max(scores, axis=-1, keepdims=True)
    p = jnp.exp(scores - top)
    p = p / jnp.sum(p, axis=-1, keepdims=True)
    p_low = p.astype(bf16)
    att = jnp.einsum("hqk,khd->qhd", p_low, v, preferred_element_type=f32)
    att = att.reshape(length, hw).astype(bf16)
    branch_att = dot_scatter(att, wo, 1, False, 1)

    mid = [mix(s_in, mix_res[0, :, j]) + depth[0, j] * branch_att for j in range(n_str)]
    unit_ff, inv_ff = norm_stats(mix(mid, mix_in[1]))
    xf = all_gather(unit_ff.astype(bf16), n_dp, 2)
    upgate = dot(xf, wf, ((1,), (0,)))
    up, gate = upgate[:, :ffl], upgate[:, ffl:]
    sig = 1.0 / (1.0 + jnp.exp(-gate))
    hidden = (gate * sig * up).astype(bf16)
    branch_ff = lax.psum_scatter(dot(hidden, ff_out, ((1,), (0,))).astype(bf16), both,
                                 scatter_dimension=0, tiled=True).astype(f32)

    d_hidden = dot(dbf, ff_out, ((1,), (1,)))
    g_ff_out = dot(hidden, dbf, ((0,), (0,)))
    d_up = d_hidden * gate * sig
    d_gate = d_hidden * up * (sig * (1.0 + gate * (1.0 - sig)))
    d_ug = jnp.concatenate([d_up, d_gate], axis=1).astype(bf16)
    d_unit = dot_scatter(d_ug, wf, n_dp, True, 3)
    g_wf = dot(xf, d_ug, ((0,), (0,))).astype(bf16).reshape(n_all, rows, 2 * ffl)
    g_wf = lax.all_to_all(g_wf, both, 0, 0, tiled=True)
    g_ff_proj = g_wf.reshape(n_all, rows, 2, ffl).transpose(1, 2, 0, 3).reshape(ff_proj.shape).astype(f32)
    d_mix_ff = norm_back(d_unit, unit_ff, inv_ff)

    d_mid = [mix(cot, mix_res[1, i]) + mix_in[1, i] * d_mix_ff for i in range(n_str)]
    d_branch_att = mix(d_mid, depth[0]).astype(bf16)
    dba = all_gather(d_branch_att, 1, 4)
    d_att = dot(dba, wo, ((1,), (1,))).astype(bf16).reshape(length, hp, HEAD_DIM)
    g_wo = dot(att, dba, ((0,), (0,))).astype(bf16)

    d_v = jnp.einsum("hqk,qhd->khd", p_low, d_att, preferred_element_type=f32)
    d_p = jnp.einsum("qhd,khd->hqk", d_att, v, preferred_element_type=f32)
    d_s = (p * (d_p - jnp.sum(p * d_p, axis=-1, keepdims=True))).astype(bf16)
    d_q = jnp.einsum("hqk,khd->qhd", d_s, k, preferred_element_type=f32) * scale
    d_k = jnp.einsum("hqk,qhd->khd", d_s, q, preferred_element_type=f32) * scale
    d_q = d_q * cosine + turn_back(d_q * sine)
    d_k = d_k * cosine + turn_back(d_k * sine)
    d_proj = jnp.stack([d_q, d_k, d_v], axis=1).reshape(length, 3 * hw).astype(bf16)
    d_unit_att = dot_scatter(d_proj, wq, 1, True, 5)
    g_wq = dot(xa, d_proj, ((0,), (0,))).astype(bf16)
    d_mix_att = norm_back(d_unit_att, unit_att, inv_att)

    g_in = [mix(d_mid, mix_res[0, i]) + mix_in[0, i] * d_mix_att for i in range(n_str)]
    out = [mix(mid, mix_res[1, :, j]) + depth[1, j] * branch_ff for j in range(n_str)]

    def inner(a, b):
        return jnp.sum(a * b)

    sums = [inner(s, d_mix_att) for s in s_in] + [inner(m, d_mix_ff) for m in mid]
    sums += [inner(s, d) for s in s_in for d in d_mid] + [inner(m, c) for m in mid for c in cot]
    sums += [inner(branch_att, d) for d in d_mid] + [inner(branch_ff, c) for c in cot]
    small = jnp.pad(jnp.stack(sums), (0, 1024 - len(sums))).reshape(8, 128)
    g_att_proj, g_attn_out, small = tail_exchange(g_wq, g_wo, small, n_dp, 6)
    small = small.reshape(-1)
    g_mix_in = small[:8].reshape(2, 4)
    g_mix_res = small[8:40].reshape(2, 4, 4)
    g_depth = small[40:48].reshape(2, 4)
    return (jnp.stack(out, axis=1).astype(bf16)[None], jnp.stack(g_in, axis=1)[None],
            g_att_proj, g_attn_out, g_ff_proj, g_ff_out, g_mix_in, g_mix_res, g_depth)


def solution(mesh):
    n_dp, n_seq = mesh.shape["dp"], mesh.shape["seq"]
    tok = P("dp", "seq", None, None)
    ids = P("dp", "seq")
    mat = P(("dp", "seq"), None)

    body = fast_body if (n_dp, n_seq) == (4, 8) else plain_body

    def run(*args):
        return body(n_dp, n_seq, *args)

    return jax.shard_map(
        run, mesh=mesh,
        in_specs=(tok, ids, ids, mat, mat, mat, mat, P(), P(), P(), tok),
        out_specs=(tok, tok, mat, mat, mat, mat, P(), P(), P()),
        check_vma=False)
```

```python
import functools

import jax
import jax.numpy as jnp
from jax import lax
from jax.experimental import pallas as pl
from jax.experimental.pallas import tpu as pltpu
from jax.sharding import PartitionSpec as P

HEADS = 16
HEAD_DIM = 128

ln_eps = 1e-05
rope_base = 10000.0
neg_big = -1e30
f32 = jnp.float32
bf16 = jnp.bfloat16


MESH = pl.DeviceIdType.MESH
DMA = pltpu.SemaphoreType.DMA
ANY = pl.BlockSpec(memory_space=pl.ANY)
VM = pl.BlockSpec(memory_space=pltpu.VMEM)

def greet(peers):
    bar = pltpu.get_barrier_semaphore()
    for p in peers:
        pl.semaphore_signal(bar, inc=1, device_id=p, device_id_type=MESH)
    pl.semaphore_wait(bar, len(peers))

def remote(src, dst, ss, rs, dev):
    return pltpu.make_async_remote_copy(src_ref=src, dst_ref=dst, send_sem=ss, recv_sem=rs, device_id=dev, device_id_type=MESH)

def place():
    z = lax.axis_index("dp"); s = lax.axis_index("seq")
    c = s // 2; k = lax.rem(s, 2)
    xc = c + 1 - 2 * lax.rem(c, 2)
    yc = lax.rem(c + 2, 4)
    dc = lax.rem(xc + 2, 4)
    return z, s, c, k, xc, yc, dc

def add_rows(dst, srcs, first, count, step=16):
    def one(i, _):
        rows = pl.ds(pl.multiple_of(first + i * step, step), step)
        total = srcs[0][rows, :].astype(f32)
        for src in srcs[1:]:
            total = total + src[rows, :].astype(f32)
        dst[rows, :] = total.astype(dst.dtype)
        return 0
    lax.fori_loop(0, count // step, one, 0)

class Gather:
    def __init__(self, nz, x, out, sems):
        self.zs, self.zr, self.cs, self.cr, self.ds, self.dr, self.ps, self.pr, self.ls = sems
        self.nz, self.x, self.out = nz, x, out
        self.z, self.s, self.c, self.k, self.xc, self.yc, self.dc = place()
        z, s, k = self.z, self.s, self.k
        self.half = x.shape[0] // 2
        self.zt = [(lax.rem(z + i, nz), s) for i in range(1, nz)]
        self.dev = [(z, 2 * self.xc + k), (z, 2 * self.yc + k)]
        self.partner = (z, s + 1 - 2 * k)
        self.src = [z] + [lax.rem(z + nz - i, nz) for i in range(1, nz)]
        self.sends = []
        self.np = 0
        self.nw = 0

    def peers(self):
        return self.zt + self.dev + [self.partner]

    def at(self, zi, chip, core, part=None):
        idx = (chip, core) if self.nz == 1 else (self.src[zi], chip, core)
        if part is not None:
            idx = idx + (pl.ds(part * self.half, self.half),)
        return self.out.at[idx]

    def go(self, *args):
        d = remote(*args)
        d.start()
        self.sends.append(d)

    def pair(self, src, dst):
        self.go(src, dst, self.ps.at[self.np], self.pr.at[self.np], self.partner)
        self.np += 1

    def plane(self, zi, src, dst):
        for j in range(2):
            self.go(src, dst, self.cs.at[zi, j], self.cr.at[zi, j], self.dev[j])

    def begin(self):
        own = self.at(0, self.c, self.k)
        self.local = pltpu.make_async_copy(self.x, own, self.ls)
        self.local.start()
        self.plane(0, self.x, own)
        for i in range(1, self.nz):
            self.go(self.x, own, self.zs.at[i - 1], self.zr.at[i - 1], self.zt[i - 1])
        self.pair(self.x, own)

    def line(self, zi):
        blk = self.at(zi, self.c, self.k)
        remote(blk, blk, self.zs.at[zi - 1], self.zr.at[zi - 1], self.zt[zi - 1]).wait_recv()
        self.plane(zi, blk, blk)
        self.pair(blk, blk)

    def near(self, zi, j):
        chip = (self.xc, self.yc)[j]
        blk = self.at(zi, chip, self.k)
        remote(blk, blk, self.cs.at[zi, j], self.cr.at[zi, j], self.dev[j]).wait_recv()
        part = self.at(zi, chip, self.k, j)
        self.go(part, part, self.ds.at[zi, j], self.dr.at[zi, j], self.dev[1 - j])
        self.pair(blk, blk)

    def far(self, zi, h):
        part = self.at(zi, self.dc, self.k, h)
        remote(part, part, self.ds.at[zi, h], self.dr.at[zi, h], self.dev[1 - h]).wait_recv()
        self.pair(part, part)

    def wait_pair(self, blk):
        remote(blk, blk, self.ps.at[self.nw], self.pr.at[self.nw], self.partner).wait_recv()
        self.nw += 1

    def steps(self):
        nz = self.nz
        other = 1 - self.k
        todo = []
        for t in range(nz + 2):
            if 1 <= t < nz:
                todo.append((lambda t=t: self.line(t), lambda t=t: self.at(t, self.c, other)))
            u = t - 1 if nz > 1 else t
            if 0 <= u < nz:
                for j in range(2):
                    todo.append((lambda u=u, j=j: self.near(u, j), lambda u=u, j=j: self.at(u, (self.xc, self.yc)[j], other)))
            u = u - 1
            if 0 <= u < nz:
                for h in range(2):
                    todo.append((lambda u=u, h=h: self.far(u, h), lambda u=u, h=h: self.at(u, self.dc, other, h)))
        return todo

    def finish(self, todo):
        self.wait_pair(self.at(0, self.c, 1 - self.k))
        for _, blk in todo:
            self.wait_pair(blk())
        for d in self.sends:
            d.wait_send()
        self.local.wait()


def gather_sems(nz):
    m = max(nz - 1, 1)
    return [DMA((m,)), DMA((m,)), DMA((nz, 2)), DMA((nz, 2)), DMA((nz, 2)), DMA((nz, 2)),
            DMA((nz * 5,)), DMA((nz * 5,)), DMA]


def gather_kernel(nz, x, out, *sems):
    g = Gather(nz, x, out, sems)
    greet(g.peers())
    g.begin()
    todo = g.steps()
    for act, _ in todo:
        act()
    g.finish(todo)


def all_gather(x, nz, cid):
    rows, width = x.shape
    shape = (4, 2, rows, width) if nz == 1 else (nz, 4, 2, rows, width)
    out = pl.pallas_call(
        functools.partial(gather_kernel, nz),
        out_shape=jax.ShapeDtypeStruct(shape, x.dtype), in_specs=[ANY], out_specs=ANY,
        scratch_shapes=gather_sems(nz),
        compiler_params=pltpu.CompilerParams(collective_id=cid, has_side_effects=True))(x)
    return out.reshape(8 * nz * rows, width)


def head_kernel(n_dp, x, ids, wp, wo, xa, ids_all, wq, wo_mine, *sems):
    gs = sems[:9]
    i_s, i_r, q_s, q_r, u_s, u_r, v_s, v_r, o_s, o_r, l_s = sems[9:]
    z, s, c, k, xc, yc, dc = place()
    n_seq = 8
    rows = wp.shape[0]
    w = wp.shape[1] // (3 * n_seq)
    me = z * n_seq + s
    g = Gather(1, x, xa, gs)
    everyone = []
    for i in range(1, n_dp * n_seq):
        t = lax.rem(me + i, n_dp * n_seq)
        everyone.append((t // n_seq, lax.rem(t, n_seq)))
    greet(everyone)
    sends = []
    locals_ = []

    def go(*args):
        d = remote(*args)
        d.start()
        sends.append(d)

    def piece(plane, t):
        return wq.at[pl.ds(pl.multiple_of((plane * n_seq + t) * rows, rows), rows)]

    def cols(t, j):
        return wp.at[:, pl.ds(pl.multiple_of(j * n_seq * w + t * w, w), w)]
    seqs = [lax.rem(s + i, n_seq) for i in range(n_seq)]
    back = [lax.rem(s + n_seq - i, n_seq) for i in range(n_seq)]
    mine = piece(z, s)
    for j in range(3):
        d = pltpu.make_async_copy(cols(s, j), mine.at[:, pl.ds(j * w, w)], l_s.at[j])
        d.start()
        locals_.append(d)
    for i in range(1, n_seq):
        for j in range(3):
            go(cols(seqs[i], j), mine.at[:, pl.ds(j * w, w)], q_s.at[i], q_r.at[i], (z, seqs[i]))
    for i in range(1, n_seq):
        own = ids_all.at[s]
        go(ids, own, i_s.at[i], i_r.at[i], (z, seqs[i]))
    d = pltpu.make_async_copy(ids, ids_all.at[s], l_s.at[3])
    d.start()
    locals_.append(d)
    g.begin()
    up, down = z < n_dp - 1, z > 0
    chain = []

    def send_up(h, plane, t):
        p = piece(plane, t)
        return remote(p, p, u_s.at[h, t], u_r.at[h, t], (z + 1, s))

    def send_down(h, plane, t):
        p = piece(plane, t)
        return remote(p, p, v_s.at[h, t], v_r.at[h, t], (z - 1, s))

    def first(i):
        if i == 0:
            for d in locals_[:3]:
                d.wait()
        else:
            p = piece(z, back[i])
            remote(p, p, q_s.at[i], q_r.at[i], (z, back[i])).wait_recv()
        t = back[i]

        @pl.when(up)
        def _():
            send_up(0, z, t).start()

        @pl.when(down)
        def _():
            send_down(0, z, t).start()

    def hop(h, i):
        t = lax.rem(s + n_seq - i, n_seq)

        @pl.when(z >= h)
        def _():
            send_up(h - 1, z - h, t).wait_recv()

            @pl.when(up)
            def _():
                send_up(h, z - h, t).start()

        @pl.when(z + h < n_dp)
        def _():
            send_down(h - 1, z + h, t).wait_recv()

            @pl.when(down)
            def _():
                send_down(h, z + h, t).start()
    for i in range(n_seq):
        first(i)
    dest = me // 4
    for i in range(n_dp):
        zt = lax.rem(z + i, n_dp)
        part = wo_mine.at[pl.ds(pl.multiple_of(lax.rem(me, 4) * rows, rows), rows)]
        if i == 0:
            @pl.when(dest != s)
            def _():
                remote(wo, part, o_s.at[0], o_r.at[lax.rem(me, 4)], (z, dest)).start()

            @pl.when(dest == s)
            def _():
                pltpu.make_async_copy(wo, part, l_s.at[4]).start()
        else:
            go(wo, part, o_s.at[i], o_r.at[lax.rem(me, 4)], (zt, dest))
    todo = g.steps()
    pending = [lambda h=h, i=i: hop(h, i) for h in range(1, n_dp) for i in range(n_seq)]
    for act, _ in todo:
        act()
        for p in pending[:2]:
            p()
        pending = pending[2:]
    for p in pending:
        p()
    for i in range(1, n_seq):
        own = ids_all.at[back[i]]
        remote(own, own, i_s.at[i], i_r.at[i], (z, back[i])).wait_recv()
    for t in range(4):
        src = s * 4 + t
        part = wo_mine.at[pl.ds(t * rows, rows)]

        @pl.when(src != me)
        def _():
            remote(part, part, o_s.at[0], o_r.at[t], (src // n_seq, lax.rem(src, n_seq))).wait_recv()

        @pl.when(src == me)
        def _():
            pltpu.make_async_copy(wo, part, l_s.at[4]).wait()
    g.finish(todo)
    for d in sends:
        d.wait_send()
    for d in locals_[3:]:
        d.wait()

    @pl.when(dest != s)
    def _():
        remote(wo, wo, o_s.at[0], o_r.at[0], (z, dest)).wait_send()
    for h in range(n_dp - 1):
        for i in range(n_seq):
            @pl.when((z >= h) & up)
            def _():
                send_up(h, z - h, back[i]).wait_send()

            @pl.when((z + h < n_dp) & down)
            def _():
                send_down(h, z + h, back[i]).wait_send()


def head_exchange(x, ids, wp, wo, n_dp, cid):
    rows, width = x.shape
    w = wp.shape[1] // 24
    n = n_dp * 8
    return pl.pallas_call(
        functools.partial(head_kernel, n_dp),
        out_shape=(jax.ShapeDtypeStruct((4, 2, rows, width), x.dtype),
                   jax.ShapeDtypeStruct((8,) + ids.shape, ids.dtype),
                   jax.ShapeDtypeStruct((n * wp.shape[0], 3 * w), wp.dtype),
                   jax.ShapeDtypeStruct((4 * wo.shape[0], wo.shape[1]), wo.dtype)),
        in_specs=[ANY] * 4, out_specs=(ANY,) * 4,
        scratch_shapes=gather_sems(1) + [DMA((8,)), DMA((8,)), DMA((8,)), DMA((8,)),
                                         DMA((n_dp, 8)), DMA((n_dp, 8)), DMA((n_dp, 8)), DMA((n_dp, 8)),
                                         DMA((n_dp,)), DMA((4,)), DMA((5,))],
        compiler_params=pltpu.CompilerParams(collective_id=cid, has_side_effects=True))(x, ids, wp, wo)


class Scatter:
    def __init__(self, nz, trans, a, b, out, bufs, sems):
        self.nz, self.a, self.b, self.out = nz, a, b, out
        self.pp, self.po, self.ra, self.rd, self.fx, self.fy, self.fz = bufs
        (self.p_s, self.p_r, self.d_s, self.d_r, self.x_s, self.x_r, self.y_s, self.y_r, self.z_s, self.z_r) = sems
        self.z, self.s, self.c, self.k, self.xc, self.yc, self.dc = place()
        z, s, k = self.z, self.s, self.k
        self.rows = out.shape[0]
        self.half = self.rows // 2
        self.parts = (pl.ds(0, self.half), pl.ds(self.half, self.half))
        self.partner = (z, s + 1 - 2 * k)
        self.dev_x = (z, 2 * self.xc + k)
        self.dev_y = (z, 2 * self.yc + k)
        self.zt = [lax.rem(z + i, nz) for i in range(1, nz)]
        self.dims = (((1,), (1,)), ((), ())) if trans else (((1,), (0,)), ((), ()))

    def peers(self):
        return [self.partner, self.dev_x, self.dev_y] + [(t, self.s) for t in self.zt]

    def produce(self, i, _):
        cx, cy, rows, k = lax.rem(self.c, 2), self.c // 2, self.rows, self.k
        j = lax.rem(i, 4)
        rx = jnp.where(j < 2, 1, 0)
        ry = jnp.where(lax.rem(j, 2) == 0, 1, 0) * jnp.where(j < 3, 1, 0)
        blk = cx + rx - 2 * cx * rx + 2 * (cy + ry - 2 * cy * ry)
        if self.nz > 1:
            blk = blk + lax.rem(self.z + 1 + i // 4, self.nz) * 4
        at = pl.ds(pl.multiple_of(blk * 2 * rows, 2 * rows), 2 * rows)
        both = lax.dot_general(self.a[at, :], self.b[...], self.dims, preferred_element_type=f32).astype(bf16)
        lower, upper = both[:rows], both[rows:]
        self.pp[i] = jnp.where(k == 0, upper, lower)
        self.po[i] = jnp.where(k == 0, lower, upper)
        remote(self.pp.at[i], self.ra.at[i], self.p_s.at[i], self.p_r.at[i], self.partner).start()
        return 0

    def make(self, g):
        lax.fori_loop(4 * g, 4 * g + 4, self.produce, 0)

    def first(self, zi, j):
        q = zi * 4 + j
        po, (lo, hi) = self.po, self.parts
        remote(self.ra.at[q], self.ra.at[q], self.p_s.at[q], self.p_r.at[q], self.partner).wait_recv()
        add_rows(po.at[q], [po.at[q], self.ra.at[q]], 0, self.rows)
        if j == 0:
            remote(po.at[q, lo], self.rd.at[zi, lo], self.d_s.at[zi, 0], self.d_r.at[zi, 0], self.dev_x).start()
            remote(po.at[q, hi], self.rd.at[zi, hi], self.d_s.at[zi, 1], self.d_r.at[zi, 1], self.dev_y).start()
        if j == 1:
            remote(po.at[q, lo], self.fx.at[zi, lo], self.x_s.at[zi, 0], self.x_r.at[zi, 0], self.dev_x).start()
        if j == 2:
            remote(po.at[q, hi], self.fy.at[zi, hi], self.y_s.at[zi, 1], self.y_r.at[zi, 1], self.dev_y).start()

    def second(self, zi):
        po, rd, (lo, hi) = self.po, self.rd, self.parts
        qx, qy = zi * 4 + 1, zi * 4 + 2
        remote(rd.at[zi, lo], rd.at[zi, lo], self.d_s.at[zi, 0], self.d_r.at[zi, 0], self.dev_x).wait_recv()
        add_rows(po.at[qy], [po.at[qy], rd.at[zi]], 0, self.half)
        remote(po.at[qy, lo], self.fy.at[zi, lo], self.y_s.at[zi, 0], self.y_r.at[zi, 0], self.dev_y).start()
        remote(rd.at[zi, hi], rd.at[zi, hi], self.d_s.at[zi, 1], self.d_r.at[zi, 1], self.dev_y).wait_recv()
        add_rows(po.at[qx], [po.at[qx], rd.at[zi]], self.half, self.half)
        remote(po.at[qx, hi], self.fx.at[zi, hi], self.x_s.at[zi, 1], self.x_r.at[zi, 1], self.dev_x).start()

    def third(self, zi):
        q, nz, po, fx, fy, fz = zi * 4 + 3, self.nz, self.po, self.fx, self.fy, self.fz
        for h, part in enumerate(self.parts):
            remote(fx.at[zi, part], fx.at[zi, part], self.x_s.at[zi, h], self.x_r.at[zi, h], self.dev_x).wait_recv()
            remote(fy.at[zi, part], fy.at[zi, part], self.y_s.at[zi, h], self.y_r.at[zi, h], self.dev_y).wait_recv()
        if zi < nz - 1:
            add_rows(po.at[q], [po.at[q], fx.at[zi], fy.at[zi]], 0, self.rows)
            remote(po.at[q], fz.at[zi], self.z_s.at[zi], self.z_r.at[zi], (self.zt[zi], self.s)).start()
        else:
            for i in range(nz - 1):
                remote(fz.at[i], fz.at[i], self.z_s.at[i], self.z_r.at[i], (self.zt[i], self.s)).wait_recv()
            add_rows(self.out, [po.at[q], fx.at[zi], fy.at[zi]] + [fz.at[i] for i in range(nz - 1)], 0, self.rows)

    def steps(self):
        nz = self.nz
        todo = [lambda: self.make(0)]
        for t in range(nz + 2):
            if t + 1 < nz:
                todo.append(lambda t=t: self.make(t + 1))
            if t < nz:
                todo += [lambda t=t, j=j: self.first(t, j) for j in range(4)]
            if 0 <= t - 1 < nz:
                todo.append(lambda t=t: self.second(t - 1))
            if 0 <= t - 2 < nz:
                todo.append(lambda t=t: self.third(t - 2))
        return todo

    def finish(self):
        for q in range(4 * self.nz):
            remote(self.ra.at[q], self.ra.at[q], self.p_s.at[q], self.p_r.at[q], self.partner).wait_send()
        for zi in range(self.nz):
            for h, part in enumerate(self.parts):
                for buf, a, b in ((self.rd, self.d_s, self.d_r), (self.fx, self.x_s, self.x_r), (self.fy, self.y_s, self.y_r)):
                    remote(buf.at[zi, part], buf.at[zi, part], a.at[zi, h], b.at[zi, h], self.dev_x).wait_send()
        for i in range(self.nz - 1):
            remote(self.fz.at[i], self.fz.at[i], self.z_s.at[i], self.z_r.at[i], self.dev_x).wait_send()


def scatter_bufs(nz, rows, width):
    m = max(nz - 1, 1)
    return [pltpu.VMEM((n, rows, width), bf16) for n in (4 * nz, 4 * nz, 4 * nz, nz, nz, nz, m)]


def scatter_sems(nz):
    m = max(nz - 1, 1)
    return [DMA((4 * nz,)), DMA((4 * nz,))] + [DMA((nz, 2))] * 6 + [DMA((m,)), DMA((m,))]


def params(cid, mib):
    return pltpu.CompilerParams(collective_id=cid, has_side_effects=True, vmem_limit_bytes=mib * 1024 * 1024)


def scatter_gather_kernel(nz, trans, a, b, x, out, xg, *rest):
    bufs, sems, gs = rest[:7], rest[7:17], rest[17:]
    sc = Scatter(1, trans, a, b, out, bufs, sems)
    g = Gather(nz, x, xg, gs)
    greet(g.peers())
    todo = g.steps()
    sc_todo = sc.steps()
    sc_todo[0]()
    g.begin()
    rest_ = sc_todo[1:]
    for act, _ in todo:
        if rest_:
            rest_.pop(0)()
        act()
    for act in rest_:
        act()
    sc.finish()
    g.finish(todo)


def scatter_gather(a, b, x, nz, trans, cid):
    rows, width = x.shape
    out, xg = pl.pallas_call(
        functools.partial(scatter_gather_kernel, nz, trans),
        out_shape=(jax.ShapeDtypeStruct((rows, width), f32), jax.ShapeDtypeStruct((nz, 4, 2, rows, width), x.dtype)),
        in_specs=[VM, VM, ANY], out_specs=(VM, ANY),
        scratch_shapes=scatter_bufs(1, rows, width) + scatter_sems(1) + gather_sems(nz),
        compiler_params=params(cid, 48))(a, b, x)
    return out, xg.reshape(nz * 8 * rows, width)


class Owners:
    def __init__(self, n_dp, gq, go, out_q, out_o, bufs, sems):
        self.n_dp, self.gq, self.go, self.out_q, self.out_o = n_dp, gq, go, out_q, out_o
        self.dn, self.up, self.st, self.rq, self.ro = bufs
        (self.dn_s, self.dn_r, self.up_s, self.up_r, self.q_s, self.q_r, self.o_s, self.o_r, self.l_s) = sems
        self.z, self.s = lax.axis_index("dp"), lax.axis_index("seq")
        self.rows = out_q.shape[0]
        self.w = out_q.shape[1] // 24
        self.me = self.z * 8 + self.s

    def part(self, plane, t):
        return self.gq.at[pl.ds(pl.multiple_of((plane * 8 + t) * self.rows, self.rows), self.rows)]

    def piece(self, i):
        return lax.rem(self.s + i, 8)

    def down(self, h, i):
        z = self.z
        own = self.part(z - h, self.piece(i))
        if h < self.n_dp - 1:
            @pl.when((z >= h) & (z < self.n_dp - 1))
            def _():
                buf = self.dn.at[h, i]
                remote(buf, buf, self.dn_s.at[h, i], self.dn_r.at[h, i], (z + 1, self.s)).wait_recv()
                add_rows(buf, [own, buf], 0, self.rows)
                remote(buf, self.dn.at[h - 1, i], self.dn_s.at[h - 1, i], self.dn_r.at[h - 1, i], (z - 1, self.s)).start()

        @pl.when((z >= h) & (z == self.n_dp - 1))
        def _():
            remote(own, self.dn.at[h - 1, i], self.dn_s.at[h - 1, i], self.dn_r.at[h - 1, i], (z - 1, self.s)).start()

    def rise(self, h, i):
        z = self.z
        own = self.part(z + h, self.piece(i))
        if h < self.n_dp - 1:
            @pl.when((z + h < self.n_dp) & (z > 0))
            def _():
                buf = self.up.at[h, i]
                remote(buf, buf, self.up_s.at[h, i], self.up_r.at[h, i], (z - 1, self.s)).wait_recv()
                add_rows(buf, [own, buf], 0, self.rows)
                remote(buf, self.up.at[h - 1, i], self.up_s.at[h - 1, i], self.up_r.at[h - 1, i], (z + 1, self.s)).start()

        @pl.when((z + h < self.n_dp) & (z == 0))
        def _():
            remote(own, self.up.at[h - 1, i], self.up_s.at[h - 1, i], self.up_r.at[h - 1, i], (z + 1, self.s)).start()

    def target(self, t):
        d = self.s * 4 + t
        return d, (d // 8, lax.rem(d, 8))

    def begin(self):
        for t in range(4):
            d, dev = self.target(t)
            src = self.go.at[pl.ds(t * self.rows, self.rows)]

            @pl.when(d != self.me)
            def _():
                remote(src, self.ro.at[self.z], self.o_s.at[t], self.o_r.at[self.z], dev).start()

            @pl.when(d == self.me)
            def _():
                pltpu.make_async_copy(src, self.ro.at[self.z], self.l_s).start()

    def last(self, i):
        z, s = self.z, self.s
        dst = self.rq.at[0] if i == 0 else self.st.at[i]
        own = self.part(z, self.piece(i))
        dn, up = self.dn.at[0, i], self.up.at[0, i]

        @pl.when(z < self.n_dp - 1)
        def _():
            remote(dn, dn, self.dn_s.at[0, i], self.dn_r.at[0, i], (z + 1, s)).wait_recv()

        @pl.when(z > 0)
        def _():
            remote(up, up, self.up_s.at[0, i], self.up_r.at[0, i], (z - 1, s)).wait_recv()

        @pl.when((z > 0) & (z < self.n_dp - 1))
        def _():
            add_rows(dst, [own, dn, up], 0, self.rows)

        @pl.when(z == 0)
        def _():
            add_rows(dst, [own, dn], 0, self.rows)

        @pl.when(z == self.n_dp - 1)
        def _():
            add_rows(dst, [own, up], 0, self.rows)
        if i:
            remote(dst, self.rq.at[i], self.q_s.at[i], self.q_r.at[i], (z, self.piece(i))).start()

    def steps(self):
        order = list(range(1, 8)) + [0]
        todo = []
        for h in range(self.n_dp - 1, 0, -1):
            for i in order:
                todo.append(lambda h=h, i=i: (self.down(h, i), self.rise(h, i)))
        todo += [lambda i=i: self.last(i) for i in order]
        return todo

    def finish(self):
        z, s, me, w = self.z, self.s, self.me, self.w
        for t in range(self.n_dp):
            from_s = me // 4

            @pl.when((z != t) | (s != from_s))
            def _():
                remote(self.ro.at[t], self.ro.at[t], self.o_s.at[0], self.o_r.at[t], (t, from_s)).wait_recv()

            @pl.when((z == t) & (s == from_s))
            def _():
                pltpu.make_async_copy(self.ro.at[t], self.ro.at[t], self.l_s).wait()
        add_rows(self.out_o, [self.ro.at[t] for t in range(self.n_dp)], 0, self.rows)
        for i in range(8):
            src = lax.rem(s + 8 - i, 8)
            if i:
                remote(self.rq.at[i], self.rq.at[i], self.q_s.at[i], self.q_r.at[i], (z, src)).wait_recv()
            for j in range(3):
                at = pl.ds(pl.multiple_of(j * 8 * w + src * w, w), w)
                self.out_q[:, at] = self.rq[i, :, j * w:(j + 1) * w].astype(f32)
        for i in range(1, 8):
            remote(self.rq.at[i], self.rq.at[i], self.q_s.at[i], self.q_r.at[i], (z, s + 1 - 2 * lax.rem(s, 2))).wait_send()
        for t in range(4):
            d, dev = self.target(t)

            @pl.when(d != me)
            def _():
                remote(self.ro.at[0], self.ro.at[0], self.o_s.at[t], self.o_r.at[0], dev).wait_send()
        for h in range(1, self.n_dp):
            for i in range(8):
                @pl.when(z >= h)
                def _():
                    buf = self.dn.at[h - 1, i]
                    remote(buf, buf, self.dn_s.at[h - 1, i], self.dn_r.at[h - 1, i], (z - 1, s)).wait_send()

                @pl.when(z + h < self.n_dp)
                def _():
                    buf = self.up.at[h - 1, i]
                    remote(buf, buf, self.up_s.at[h - 1, i], self.up_r.at[h - 1, i], (z + 1, s)).wait_send()


def everyone():
    z, s = lax.axis_index("dp"), lax.axis_index("seq")
    n = lax.axis_size("dp") * 8
    found = []
    for i in range(1, n):
        t = lax.rem(z * 8 + s + i, n)
        found.append((t // 8, lax.rem(t, 8)))
    return found


def final_kernel(n_dp, hid, wo, dp_, wq, gq, go, bf, dua, out_q, out_o, *rest):
    s4, s1, own = rest[:17], rest[17:34], rest[34:]
    big = Scatter(n_dp, False, hid, wo, bf, s4[:7], s4[7:])
    near = Scatter(1, True, dp_, wq, dua, s1[:7], s1[7:])
    grads = Owners(n_dp, gq, go, out_q, out_o, own[:5], own[5:])
    greet(everyone())
    lists = [grads.steps(), big.steps(), near.steps()]
    lists[1].pop(0)()
    for act in lists[0][:8]:
        act()
    grads.begin()
    lists[0] = lists[0][8:]
    lists[2].pop(0)()
    while any(lists):
        if lists[1]:
            lists[1].pop(0)()
        if lists[2] and len(lists[1]) < 20:
            lists[2].pop(0)()
        if lists[0]:
            lists[0].pop(0)()
    big.finish()
    near.finish()
    grads.finish()


def final_exchange(hid, wo, d_proj, wq, gq, gwo, n_dp, cid):
    n = n_dp * 8
    width = wo.shape[1]
    rows, w3 = gq.shape[0] // n, gq.shape[1]
    toks = hid.shape[0] // n
    blk = lambda *k: pltpu.VMEM(k + (rows, w3), bf16)
    h = n_dp - 1
    return pl.pallas_call(
        functools.partial(final_kernel, n_dp),
        out_shape=(jax.ShapeDtypeStruct((toks, width), f32), jax.ShapeDtypeStruct((toks, width), f32),
                   jax.ShapeDtypeStruct((rows, w3 * 8), f32), jax.ShapeDtypeStruct((rows, width), f32)),
        in_specs=[VM] * 6, out_specs=(VM,) * 4,
        scratch_shapes=scatter_bufs(n_dp, toks, width) + scatter_sems(n_dp) + scatter_bufs(1, toks, width) + scatter_sems(1)
        + [blk(h, 8), blk(h, 8), blk(8), blk(8), pltpu.VMEM((n_dp, rows, width), bf16)]
        + [DMA((h, 8))] * 4 + [DMA((8,)), DMA((8,)), DMA((4,)), DMA((n_dp,)), DMA],
        compiler_params=params(cid, 63))(hid, wo, d_proj, wq, gq, gwo)


def total_kernel(n_dp, x, out, rs, m_s, m_r):
    devs = everyone()
    greet(devs)
    sends = []
    for i, dev in enumerate(devs):
        d = remote(x, rs.at[i], m_s.at[i], m_r.at[i], dev)
        d.start()
        sends.append(d)
    total = x[...]
    for i in range(len(devs)):
        remote(rs.at[i], rs.at[i], m_s.at[i], m_r.at[i], devs[0]).wait_recv()
        total = total + rs[i]
    out[...] = total
    for d in sends:
        d.wait_send()


def total_all(x, n_dp, cid):
    n = n_dp * 8 - 1
    return pl.pallas_call(
        functools.partial(total_kernel, n_dp), out_shape=jax.ShapeDtypeStruct(x.shape, f32),
        in_specs=[VM], out_specs=VM,
        scratch_shapes=[pltpu.VMEM((n,) + x.shape, f32), DMA((n,)), DMA((n,))],
        compiler_params=pltpu.CompilerParams(collective_id=cid, has_side_effects=True))(x)


def dot(a, b, dims):
    return lax.dot_general(a, b, (dims, ((), ())), preferred_element_type=f32)


def norm_stats(values):
    mean = jnp.mean(values, axis=-1, keepdims=True)
    centered = values - mean
    inv = lax.rsqrt(jnp.mean(centered * centered, axis=-1, keepdims=True) + ln_eps)
    return centered * inv, inv


def norm_back(grad, unit, inv):
    mean = jnp.mean(grad, axis=-1, keepdims=True)
    proj = jnp.mean(grad * unit, axis=-1, keepdims=True)
    return (grad - mean - unit * proj) * inv


def rope_tables(positions):
    half = HEAD_DIM // 2
    inv_freq = rope_base ** (-(jnp.arange(half, dtype=f32) * 2.0 / HEAD_DIM))
    angles = positions.astype(f32)[..., None] * inv_freq
    angles = jnp.concatenate([angles, angles], axis=-1)
    return jnp.cos(angles), jnp.sin(angles)


def turn(values):
    half = HEAD_DIM // 2
    return jnp.concatenate([-values[..., half:], values[..., :half]], axis=-1)


def turn_back(values):
    half = HEAD_DIM // 2
    return jnp.concatenate([values[..., half:], -values[..., :half]], axis=-1)


def ff_kernel(nz, x, dbf, wf, wo, xf, out, hid, dug, xb, gb, pp, po, ra, rd, fx, fy, fz, *sems):
    ag, rs = sems[:9], sems[9:]
    zs, zr, cs, cr, ds, dr, ps, pr, ls = ag
    p_s, p_r, d_s, d_r, x_s, x_r, y_s, y_r, z_s, z_r, l_s = rs
    z, s, c, k, xc, yc, dc = place()
    rows = x.shape[0]
    half = rows // 2
    ffl = wo.shape[0]
    partner = (z, s + 1 - 2 * k)
    dev = [(z, 2 * xc + k), (z, 2 * yc + k)]
    zt = [lax.rem(z + i, nz) for i in range(1, nz)]
    greet([partner] + dev + [(t, s) for t in zt])
    lo, hi = pl.ds(0, half), pl.ds(half, half)
    parts = (lo, hi)
    cx, cy = lax.rem(c, 2), c // 2

    def plane_of(g):
        return lax.rem(z + nz - g, nz)

    def chip_of(j):
        rx = jnp.where(j < 2, 1, 0)
        ry = jnp.where(lax.rem(j, 2) == 0, 1, 0) * jnp.where(j < 3, 1, 0)
        return cx + rx - 2 * cx * rx + 2 * (cy + ry - 2 * cy * ry)

    def pair(g, slot, blk):
        remote(blk, blk, ps.at[g, slot], pr.at[g, slot], partner).start()

    own = xf.at[z, c, k]
    local = pltpu.make_async_copy(x, own, ls)
    local.start()
    for j in range(2):
        remote(x, own, cs.at[0, j], cr.at[0, j], dev[j]).start()
    for i in range(1, nz):
        remote(x, own, zs.at[i - 1], zr.at[i - 1], (zt[i - 1], s)).start()
    remote(x, own, ps.at[0, 0], pr.at[0, 0], partner).start()
    local.wait()

    def line(g):
        blk = xf.at[plane_of(g), c, k]
        remote(blk, blk, zs.at[g - 1], zr.at[g - 1], dev[0]).wait_recv()
        for j in range(2):
            remote(blk, blk, cs.at[g, j], cr.at[g, j], dev[j]).start()
        pair(g, 0, blk)

    def near(g, j):
        blk = xf.at[plane_of(g), (xc, yc)[j], k]
        remote(blk, blk, cs.at[g, j], cr.at[g, j], dev[j]).wait_recv()
        part = xf.at[plane_of(g), (xc, yc)[j], k, parts[j]]
        remote(part, part, ds.at[g, j], dr.at[g, j], dev[1 - j]).start()
        pair(g, 1 + j, blk)

    def far(g, h):
        part = xf.at[plane_of(g), dc, k, parts[h]]
        remote(part, part, ds.at[g, h], dr.at[g, h], dev[1 - h]).wait_recv()
        pair(g, 3 + h, part)

    def compute(g, j):
        plane, chip = plane_of(g), chip_of(j)
        blk = xf.at[plane, chip, 1 - k]

        @pl.when(j == 0)
        def _():
            for h in range(2):
                part = xf.at[plane, chip, 1 - k, parts[h]]
                remote(part, part, ps.at[g, 3 + h], pr.at[g, 3 + h], partner).wait_recv()

        @pl.when(j > 0)
        def _():
            slot = jnp.where(j == 3, 0, j)
            remote(blk, blk, ps.at[g, slot], pr.at[g, slot], partner).wait_recv()
        load = pltpu.make_async_copy(xf.at[plane, chip], xb, l_s.at[0])
        load.start()
        grads = pltpu.make_async_copy(dbf.at[plane, chip], gb, l_s.at[1])
        grads.start()
        load.wait()
        rows2 = 2 * rows
        upgate = jnp.dot(xb[...].reshape(rows2, x.shape[1]), wf[...], preferred_element_type=f32)
        up, gate = upgate[:, :ffl], upgate[:, ffl:]
        sig = 1.0 / (1.0 + jnp.exp(-gate))
        act = gate * sig
        grads.wait()
        d_h = lax.dot_general(gb[...].reshape(rows2, x.shape[1]), wo[...], (((1,), (1,)), ((), ())),
                              preferred_element_type=f32)
        at = pl.ds(pl.multiple_of((plane * 4 + chip) * rows2, rows2), rows2)
        hid[at, :] = (act * up).astype(bf16)
        d_up = (d_h * act).astype(bf16)
        d_gate = (d_h * up * (sig * (1.0 + gate * (1.0 - sig)))).astype(bf16)
        both = jnp.concatenate([d_up, d_gate], axis=1)
        dug[at, :] = both
        back = lax.dot_general(both, wf[...], (((1,), (1,)), ((), ())), preferred_element_type=f32).astype(bf16)
        pp[g, j, 0] = back[:rows]
        pp[g, j, 1] = back[rows:]
        remote(pp.at[g, j, 1 - k], ra.at[g, j], p_s.at[g, j], p_r.at[g, j], partner).start()

    def first(g, j):
        remote(ra.at[g, j], ra.at[g, j], p_s.at[g, j], p_r.at[g, j], partner).wait_recv()
        mine = po.at[g, j]
        add_rows(mine, [pp.at[g, j, k], ra.at[g, j]], 0, rows)
        if j == 0:
            remote(mine.at[lo], rd.at[g, lo], d_s.at[g, 0], d_r.at[g, 0], dev[0]).start()
            remote(mine.at[hi], rd.at[g, hi], d_s.at[g, 1], d_r.at[g, 1], dev[1]).start()
        if j == 1:
            remote(mine.at[lo], fx.at[g, lo], x_s.at[g, 0], x_r.at[g, 0], dev[0]).start()
        if j == 2:
            remote(mine.at[hi], fy.at[g, hi], y_s.at[g, 1], y_r.at[g, 1], dev[1]).start()

    def second(g):
        remote(rd.at[g, lo], rd.at[g, lo], d_s.at[g, 0], d_r.at[g, 0], dev[0]).wait_recv()
        add_rows(po.at[g, 2], [po.at[g, 2], rd.at[g]], 0, half)
        remote(po.at[g, 2, lo], fy.at[g, lo], y_s.at[g, 0], y_r.at[g, 0], dev[1]).start()
        remote(rd.at[g, hi], rd.at[g, hi], d_s.at[g, 1], d_r.at[g, 1], dev[1]).wait_recv()
        add_rows(po.at[g, 1], [po.at[g, 1], rd.at[g]], half, half)
        remote(po.at[g, 1, hi], fx.at[g, hi], x_s.at[g, 1], x_r.at[g, 1], dev[0]).start()

    def third(g):
        for h, part in enumerate(parts):
            remote(fx.at[g, part], fx.at[g, part], x_s.at[g, h], x_r.at[g, h], dev[0]).wait_recv()
            remote(fy.at[g, part], fy.at[g, part], y_s.at[g, h], y_r.at[g, h], dev[1]).wait_recv()
        add_rows(po.at[g, 3], [po.at[g, 3], fx.at[g], fy.at[g]], 0, rows)

        @pl.when(g > 0)
        def _():
            remote(po.at[g, 3], fz.at[g - 1], z_s.at[g - 1], z_r.at[g - 1], (plane_of(g), s)).start()

    def turn_(t, _):
        @pl.when((t >= 1) & (t < nz))
        def _():
            line(t)

        @pl.when((t >= 1) & (t <= nz))
        def _():
            near(t - 1, 0)
            near(t - 1, 1)

        @pl.when((t >= 2) & (t <= nz + 1))
        def _():
            far(t - 2, 0)
            far(t - 2, 1)

        def some(j, _):
            g = jnp.where(j == 0, t - 2, t - 1)

            @pl.when((g >= 0) & (g < nz))
            def _():
                compute(g, j)
            return 0
        lax.fori_loop(0, 4, some, 0)

        @pl.when((t >= 1) & (t <= nz))
        def _():
            first(t - 1, 1)
            first(t - 1, 2)
            first(t - 1, 3)

        @pl.when((t >= 2) & (t <= nz + 1))
        def _():
            first(t - 2, 0)

        @pl.when((t >= 3) & (t <= nz + 2))
        def _():
            second(t - 3)

        @pl.when((t >= 4) & (t <= nz + 3))
        def _():
            third(t - 4)
        return 0
    lax.fori_loop(1, nz + 4, turn_, 0)
    for i in range(nz - 1):
        remote(fz.at[i], fz.at[i], z_s.at[i], z_r.at[i], (zt[i], s)).wait_recv()
    add_rows(out, [po.at[0, 3]] + [fz.at[i] for i in range(nz - 1)], 0, rows)
    for i in range(nz - 1):
        remote(x, x, zs.at[i], zr.at[i], partner).wait_send()
        remote(fz.at[i], fz.at[i], z_s.at[i], z_r.at[i], partner).wait_send()

    def drain(g, _):
        for j in range(2):
            remote(x, x, cs.at[g, j], cr.at[g, j], partner).wait_send()
            remote(x.at[lo], x.at[lo], ds.at[g, j], dr.at[g, j], partner).wait_send()
            for a, b in ((d_s, d_r), (x_s, x_r), (y_s, y_r)):
                remote(rd.at[g, lo], rd.at[g, lo], a.at[g, j], b.at[g, j], partner).wait_send()
            remote(x.at[lo], x.at[lo], ps.at[g, 3 + j], pr.at[g, 3 + j], partner).wait_send()
        for j in range(3):
            remote(x, x, ps.at[g, j], pr.at[g, j], partner).wait_send()
        for j in range(4):
            remote(ra.at[g, j], ra.at[g, j], p_s.at[g, j], p_r.at[g, j], partner).wait_send()
        return 0
    lax.fori_loop(0, nz, drain, 0)


def feed_forward(x, dbf, wf, wo, nz, cid):
    rows, width = x.shape
    ffl = wo.shape[0]
    toks = rows * 8 * nz
    blk = lambda *n: pltpu.VMEM(n + (rows, width), bf16)
    sem = lambda *n: DMA(n)
    xf, d_unit, hidden, d_ug = pl.pallas_call(
        functools.partial(ff_kernel, nz),
        out_shape=(jax.ShapeDtypeStruct((nz, 4, 2, rows, width), bf16), jax.ShapeDtypeStruct((rows, width), f32),
                   jax.ShapeDtypeStruct((toks, ffl), bf16), jax.ShapeDtypeStruct((toks, 2 * ffl), bf16)),
        in_specs=[ANY, ANY, VM, VM], out_specs=(ANY, VM, VM, VM),
        scratch_shapes=[blk(2), blk(2), blk(nz, 4, 2), blk(nz, 4), blk(nz, 4), blk(nz), blk(nz), blk(nz), blk(nz - 1),
                        sem(nz - 1), sem(nz - 1), sem(nz, 2), sem(nz, 2), sem(nz, 2), sem(nz, 2), sem(nz, 5), sem(nz, 5), DMA,
                        sem(nz, 4), sem(nz, 4), sem(nz, 2), sem(nz, 2), sem(nz, 2), sem(nz, 2), sem(nz, 2), sem(nz, 2),
                        sem(nz - 1), sem(nz - 1), sem(2)],
        compiler_params=pltpu.CompilerParams(collective_id=cid, has_side_effects=True,
                                             vmem_limit_bytes=62 * 1024 * 1024),
    )(x, dbf.reshape(nz, 4, 2, rows, width), wf, wo)
    return xf.reshape(toks, width), d_unit, hidden, d_ug


SM = pl.BlockSpec(memory_space=pltpu.SMEM)


def combine(parts, weights):
    total = parts[0] * weights[0]
    for part, weight in zip(parts[1:], weights[1:]):
        total = total + part * weight
    return total


def row(ref, i):
    return [ref[i, j] for j in range(4)]


def planes(ref):
    return [ref[i].astype(f32) for i in range(4)]


def scalar_table(mix_in, mix_res, depth):
    through_in = jnp.sum(mix_res[0] * mix_in[1][None, :], axis=1)
    through_depth = jnp.sum(mix_res[1] * depth[0][:, None], axis=0)
    cross = jnp.sum(mix_res[0][:, :, None] * mix_res[1][None], axis=1)
    dot_ = jnp.sum(depth[0] * mix_in[1])
    return jnp.concatenate([mix_in[:1], through_in[None], through_depth[None], depth[1:],
                            jnp.broadcast_to(dot_, (1, 4)), cross], axis=0)


def pre_kernel(tab, st, ct, xn, db, so, co):
    s_in = [st[0, :, i, :] for i in range(4)]
    cot = [ct[0, :, i, :] for i in range(4)]
    for i in range(4):
        so[i] = s_in[i]
        co[i] = cot[i]
    unit, _ = norm_stats(combine([v.astype(f32) for v in s_in], row(tab, 0)))
    xn[...] = unit.astype(bf16)
    db[...] = combine([v.astype(f32) for v in cot], row(tab, 3)).astype(bf16)


def mixed_ff(tab, s_in, branch):
    return norm_stats(combine(s_in, row(tab, 1)) + tab[4, 0] * branch)


def mid_kernel(tab, st, ba, xn):
    unit, _ = mixed_ff(tab, planes(st), ba[...])
    xn[...] = unit.astype(bf16)


def back_kernel(tab, st, ct, ba, du, dba):
    unit, inv = mixed_ff(tab, planes(st), ba[...])
    d_mix = norm_back(du[...], unit, inv)
    dba[...] = (combine(planes(ct), row(tab, 2)) + tab[4, 0] * d_mix).astype(bf16)


def end_kernel(tab, mi, dep, st, ct, ba, bf, duf, dua, out, gs, small, acc):
    s_in, cot = planes(st), planes(ct)
    b_att, b_ff = ba[...], bf[...]
    unit, inv = mixed_ff(tab, s_in, b_att)
    d_ff = norm_back(duf[...], unit, inv)
    unit, inv = norm_stats(combine(s_in, row(tab, 0)))
    d_att = norm_back(dua[...], unit, inv)
    for i in range(4):
        gs[0, :, i, :] = combine(cot, row(tab, 5 + i)) + tab[1, i] * d_ff + tab[0, i] * d_att
        out[0, :, i, :] = (combine(s_in, [tab[5 + k, i] for k in range(4)]) + tab[2, i] * b_att
                           + tab[3, i] * b_ff).astype(bf16)
    pairs = [(s, c) for s in s_in for c in cot] + [(s, d_ff) for s in s_in] + [(s, d_att) for s in s_in]
    pairs += [(b_att, c) for c in cot] + [(b_ff, c) for c in cot] + [(b_att, d_ff)]

    @pl.when(pl.program_id(0) == 0)
    def _():
        acc[...] = jnp.zeros_like(acc)
    for q, (a, b) in enumerate(pairs):
        product = a * b
        total = product[:, :128]
        for j in range(1, product.shape[1] // 128):
            total = total + product[:, j * 128:(j + 1) * 128]
        acc[q] += total

    @pl.when(pl.program_id(0) == pl.num_programs(0) - 1)
    def _():
        small[...] = jnp.sum(acc[...], axis=1)


def small_grads(sums, mix_in, mix_res, depth):
    s_c, s_f, s_a = sums[:16].reshape(4, 4), sums[16:20], sums[20:24]
    b_c, bf_c, b_f = sums[24:28], sums[28:32], sums[32]
    mm = lambda a, b: jnp.sum(a[:, :, None] * b[None], axis=1)
    in_ff = jnp.sum(mix_res[0] * s_f[:, None], axis=0) + depth[0] * b_f
    res_ff = mm(mix_res[0].T, s_c) + depth[0][:, None] * b_c[None]
    res_att = mm(s_c, mix_res[1].T) + s_f[:, None] * mix_in[1][None]
    depth_att = jnp.sum(mix_res[1] * b_c[None], axis=1) + mix_in[1] * b_f
    return jnp.stack([s_a, in_ff]), jnp.stack([res_att, res_ff]), jnp.stack([depth_att, bf_c])


def token_call(kernel, scalars, arrays, outs, scratch=(), step=16):
    toks, width = [a for a in arrays if a.ndim == 2 or a.ndim == 4][0].shape[-2:] if arrays[0].ndim != 4 else (
        arrays[0].shape[1], arrays[0].shape[3])
    specs_of = {
        "tok": ((1, toks, 4, width), pl.BlockSpec((1, step, 4, width), lambda i: (0, i, 0, 0))),
        "mat": ((toks, width), pl.BlockSpec((step, width), lambda i: (i, 0))),
        "pla": ((4, toks, width), pl.BlockSpec((4, step, width), lambda i: (0, i, 0))),
        "sum": ((40, 128), pl.BlockSpec((40, 128), lambda i: (0, 0)))}
    kind_of = {4: "tok", 3: "pla", 2: "mat"}
    return pl.pallas_call(
        kernel, grid=(toks // step,),
        out_shape=tuple(jax.ShapeDtypeStruct(specs_of[kind][0], dtype) for kind, dtype in outs),
        out_specs=tuple(specs_of[kind][1] for kind, _ in outs),
        in_specs=[SM] * len(scalars) + [specs_of[kind_of[a.ndim]][1] for a in arrays],
        scratch_shapes=list(scratch),
        compiler_params=pltpu.CompilerParams(vmem_limit_bytes=48 * 1024 * 1024),
    )(*scalars, *arrays)


def plain_body(n_dp, n_seq, streams, segments, positions, att_proj, attn_out, ff_proj, ff_out,
         mix_in, mix_res, depth, cotangent):
    seq_count, toks, n_str, width = streams.shape
    assert seq_count == 1
    n_all = n_dp * n_seq
    both = ("dp", "seq")
    rows = att_proj.shape[0]
    ffl = ff_out.shape[0]
    hp = HEADS // n_seq
    hw = hp * HEAD_DIM
    length = toks * n_seq
    scale = HEAD_DIM ** -0.5
    seq_id = lax.axis_index("seq")

    def mix(parts, weights):
        total = parts[0] * weights[0]
        for i in range(1, n_str):
            total = total + parts[i] * weights[i]
        return total

    wq = att_proj.reshape(rows, 3, n_seq, hw)
    wq = lax.all_to_all(wq, "seq", 2, 0, tiled=True).reshape(n_seq * rows, 3 * hw)
    wq = lax.all_gather(wq, "dp", axis=0, tiled=True)
    wf = ff_proj.reshape(rows, 2, n_all, ffl)
    wf = lax.all_to_all(wf, both, 2, 0, tiled=True).reshape(n_all * rows, 2 * ffl)
    wo = lax.all_gather(attn_out, both, axis=0, tiled=True)
    wo = lax.dynamic_slice_in_dim(wo, seq_id * hw, hw, 0)
    seg_all = lax.all_gather(segments[0], "seq", axis=0, tiled=True)
    pos_all = lax.all_gather(positions[0], "seq", axis=0, tiled=True)

    s_in = [streams[0, :, i].astype(f32) for i in range(n_str)]
    cot = [cotangent[0, :, i].astype(f32) for i in range(n_str)]
    d_branch_ff = mix(cot, depth[1]).astype(bf16)
    dbf = lax.all_gather(d_branch_ff, both, axis=0, tiled=True)

    unit_att, inv_att = norm_stats(mix(s_in, mix_in[0]))
    xa = lax.all_gather(unit_att.astype(bf16), "seq", axis=0, tiled=True)
    proj = dot(xa, wq, ((1,), (0,))).reshape(length, 3, hp, HEAD_DIM)
    cosine, sine = rope_tables(pos_all)
    cosine, sine = cosine[:, None], sine[:, None]
    q = (proj[:, 0] * cosine + turn(proj[:, 0]) * sine).astype(bf16)
    k = (proj[:, 1] * cosine + turn(proj[:, 1]) * sine).astype(bf16)
    v = proj[:, 2].astype(bf16)
    idx = jnp.arange(length, dtype=jnp.int32)
    allowed = (idx[None, :] <= idx[:, None]) | (
        (seg_all[None, :] == seg_all[:, None]) & (seg_all[:, None] > 0))
    scores = jnp.einsum("qhd,khd->hqk", q, k, preferred_element_type=f32) * scale
    scores = jnp.where(allowed[None], scores, neg_big)
    top = jnp.max(scores, axis=-1, keepdims=True)
    p = jnp.exp(scores - top)
    p = p / jnp.sum(p, axis=-1, keepdims=True)
    p_low = p.astype(bf16)
    att = jnp.einsum("hqk,khd->qhd", p_low, v, preferred_element_type=f32)
    att = att.reshape(length, hw).astype(bf16)
    branch_att = lax.psum_scatter(dot(att, wo, ((1,), (0,))).astype(bf16), "seq",
                                  scatter_dimension=0, tiled=True).astype(f32)

    mid = [mix(s_in, mix_res[0, :, j]) + depth[0, j] * branch_att for j in range(n_str)]
    unit_ff, inv_ff = norm_stats(mix(mid, mix_in[1]))
    xf = lax.all_gather(unit_ff.astype(bf16), both, axis=0, tiled=True)
    upgate = dot(xf, wf, ((1,), (0,)))
    up, gate = upgate[:, :ffl], upgate[:, ffl:]
    sig = 1.0 / (1.0 + jnp.exp(-gate))
    hidden = (gate * sig * up).astype(bf16)
    branch_ff = lax.psum_scatter(dot(hidden, ff_out, ((1,), (0,))).astype(bf16), both,
                                 scatter_dimension=0, tiled=True).astype(f32)

    d_hidden = dot(dbf, ff_out, ((1,), (1,)))
    g_ff_out = dot(hidden, dbf, ((0,), (0,)))
    d_up = d_hidden * gate * sig
    d_gate = d_hidden * up * (sig * (1.0 + gate * (1.0 - sig)))
    d_ug = jnp.concatenate([d_up, d_gate], axis=1).astype(bf16)
    d_unit = lax.psum_scatter(dot(d_ug, wf, ((1,), (1,))).astype(bf16), both,
                              scatter_dimension=0, tiled=True).astype(f32)
    g_wf = dot(xf, d_ug, ((0,), (0,))).astype(bf16).reshape(n_all, rows, 2 * ffl)
    g_wf = lax.all_to_all(g_wf, both, 0, 0, tiled=True)
    g_ff_proj = g_wf.reshape(n_all, rows, 2, ffl).transpose(1, 2, 0, 3).reshape(ff_proj.shape).astype(f32)
    d_mix_ff = norm_back(d_unit, unit_ff, inv_ff)

    d_mid = [mix(cot, mix_res[1, i]) + mix_in[1, i] * d_mix_ff for i in range(n_str)]
    d_branch_att = mix(d_mid, depth[0]).astype(bf16)
    dba = lax.all_gather(d_branch_att, "seq", axis=0, tiled=True)
    d_att = dot(dba, wo, ((1,), (1,))).astype(bf16).reshape(length, hp, HEAD_DIM)
    g_wo = dot(att, dba, ((0,), (0,))).astype(bf16)
    g_wo = lax.all_gather(g_wo, "seq", axis=0, tiled=True)
    g_attn_out = lax.psum_scatter(g_wo, "dp", scatter_dimension=0, tiled=True)
    g_attn_out = lax.dynamic_slice_in_dim(g_attn_out, seq_id * rows, rows, 0).astype(f32)

    d_v = jnp.einsum("hqk,qhd->khd", p_low, d_att, preferred_element_type=f32)
    d_p = jnp.einsum("qhd,khd->hqk", d_att, v, preferred_element_type=f32)
    d_s = (p * (d_p - jnp.sum(p * d_p, axis=-1, keepdims=True))).astype(bf16)
    d_q = jnp.einsum("hqk,khd->qhd", d_s, k, preferred_element_type=f32) * scale
    d_k = jnp.einsum("hqk,qhd->khd", d_s, q, preferred_element_type=f32) * scale
    d_q = d_q * cosine + turn_back(d_q * sine)
    d_k = d_k * cosine + turn_back(d_k * sine)
    d_proj = jnp.stack([d_q, d_k, d_v], axis=1).reshape(length, 3 * hw).astype(bf16)
    d_unit_att = lax.psum_scatter(dot(d_proj, wq, ((1,), (1,))).astype(bf16), "seq",
                                  scatter_dimension=0, tiled=True).astype(f32)
    g_wq = dot(xa, d_proj, ((0,), (0,))).astype(bf16)
    g_wq = lax.psum_scatter(g_wq, "dp", scatter_dimension=0, tiled=True)
    g_wq = lax.all_to_all(g_wq.reshape(n_seq, rows, 3 * hw), "seq", 0, 0, tiled=True)
    g_att_proj = g_wq.reshape(n_seq, rows, 3, hw).transpose(1, 2, 0, 3).reshape(att_proj.shape).astype(f32)
    d_mix_att = norm_back(d_unit_att, unit_att, inv_att)

    g_in = [mix(d_mid, mix_res[0, i]) + mix_in[0, i] * d_mix_att for i in range(n_str)]
    out = [mix(mid, mix_res[1, :, j]) + depth[1, j] * branch_ff for j in range(n_str)]

    def inner(a, b):
        return jnp.sum(a * b)

    g_mix_in = jnp.stack([
        jnp.stack([inner(s, d_mix_att) for s in s_in]),
        jnp.stack([inner(m, d_mix_ff) for m in mid])])
    g_mix_res = jnp.stack([
        jnp.stack([jnp.stack([inner(s, d) for d in d_mid]) for s in s_in]),
        jnp.stack([jnp.stack([inner(m, c) for c in cot]) for m in mid])])
    g_depth = jnp.stack([
        jnp.stack([inner(branch_att, d) for d in d_mid]),
        jnp.stack([inner(branch_ff, c) for c in cot])])
    g_mix_in, g_mix_res, g_depth = lax.psum((g_mix_in, g_mix_res, g_depth), both)
    return (jnp.stack(out, axis=1).astype(bf16)[None], jnp.stack(g_in, axis=1)[None],
            g_att_proj, g_attn_out, g_ff_proj, g_ff_out, g_mix_in, g_mix_res, g_depth)


def fast_body(n_dp, n_seq, streams, segments, positions, att_proj, attn_out, ff_proj, ff_out,
              mix_in, mix_res, depth, cotangent):
    _, toks, _, width = streams.shape
    n_all = n_dp * n_seq
    both = ("dp", "seq")
    rows = att_proj.shape[0]
    ffl = ff_out.shape[0]
    hp = HEADS // n_seq
    hw = hp * HEAD_DIM
    length = toks * n_seq
    scale = HEAD_DIM ** -0.5
    tab = scalar_table(mix_in, mix_res, depth)

    xn, d_branch_ff, s_low, c_low = token_call(
        pre_kernel, (tab,), (streams, cotangent), [("mat", bf16), ("mat", bf16), ("pla", bf16), ("pla", bf16)])

    ids = jnp.concatenate([segments, positions, jnp.zeros((6, toks), jnp.int32)], axis=0)
    wf = ff_proj.reshape(rows, 2, n_all, ffl).transpose(2, 0, 1, 3).reshape(n_all, rows, 2 * ffl)
    xa, ids_all, wq, wo = head_exchange(xn, ids, att_proj, attn_out, n_dp, 0)
    xa, ids_all, wq, wo, wf = lax.optimization_barrier((xa, ids_all, wq, wo, wf))
    wf = lax.all_to_all(wf, both, 0, 0, tiled=True).reshape(n_all * rows, 2 * ffl)
    xa = xa.reshape(length, width)
    seg_all = ids_all[:, 0].reshape(length)
    pos_all = ids_all[:, 1].reshape(length)
    proj = dot(xa, wq, ((1,), (0,))).reshape(length, 3, hp, HEAD_DIM)
    cosine, sine = rope_tables(pos_all)
    cosine, sine = cosine[:, None], sine[:, None]
    q = (proj[:, 0] * cosine + turn(proj[:, 0]) * sine).astype(bf16)
    k = (proj[:, 1] * cosine + turn(proj[:, 1]) * sine).astype(bf16)
    v = proj[:, 2].astype(bf16)
    idx = jnp.arange(length, dtype=jnp.int32)
    allowed = (idx[None, :] <= idx[:, None]) | (
        (seg_all[None, :] == seg_all[:, None]) & (seg_all[:, None] > 0))
    scores = jnp.einsum("qhd,khd->hqk", q, k, preferred_element_type=f32) * scale
    scores = jnp.where(allowed[None], scores, neg_big)
    top = jnp.max(scores, axis=-1, keepdims=True)
    p = jnp.exp(scores - top)
    p = p / jnp.sum(p, axis=-1, keepdims=True)
    p_low = p.astype(bf16)
    att = jnp.einsum("hqk,khd->qhd", p_low, v, preferred_element_type=f32)
    att = att.reshape(length, hw).astype(bf16)
    branch_att, dbf = scatter_gather(att, wo, d_branch_ff, n_dp, False, 1)

    xn_ff, = token_call(mid_kernel, (tab,), (s_low, branch_att), [("mat", bf16)])
    xf, d_unit, hidden, d_ug = feed_forward(xn_ff, dbf, wf, ff_out, n_dp, 2)
    g_wf = dot(xf, d_ug, ((0,), (0,))).astype(bf16).reshape(n_all, rows, 2 * ffl)
    g_wf = lax.all_to_all(g_wf, both, 0, 0, tiled=True)
    d_branch_att, = token_call(back_kernel, (tab,), (s_low, c_low, branch_att, d_unit), [("mat", bf16)])
    dba = all_gather(d_branch_att, 1, 4)
    d_att = dot(dba, wo, ((1,), (1,))).astype(bf16).reshape(length, hp, HEAD_DIM)
    g_wo = dot(att, dba, ((0,), (0,))).astype(bf16)

    d_v = jnp.einsum("hqk,qhd->khd", p_low, d_att, preferred_element_type=f32)
    d_p = jnp.einsum("qhd,khd->hqk", d_att, v, preferred_element_type=f32)
    d_s = (p * (d_p - jnp.sum(p * d_p, axis=-1, keepdims=True))).astype(bf16)
    d_q = jnp.einsum("hqk,khd->qhd", d_s, k, preferred_element_type=f32) * scale
    d_k = jnp.einsum("hqk,qhd->khd", d_s, q, preferred_element_type=f32) * scale
    d_q = d_q * cosine + turn_back(d_q * sine)
    d_k = d_k * cosine + turn_back(d_k * sine)
    d_proj = jnp.stack([d_q, d_k, d_v], axis=1).reshape(length, 3 * hw).astype(bf16)
    g_wq = dot(xa, d_proj, ((0,), (0,))).astype(bf16)
    branch_ff, d_unit_att, g_att_proj, g_attn_out = final_exchange(hidden, ff_out, d_proj, wq, g_wq, g_wo, n_dp, 3)
    out, g_in, small = token_call(
        end_kernel, (tab, mix_in, depth), (s_low, c_low, branch_att, branch_ff, d_unit, d_unit_att),
        [("tok", bf16), ("tok", f32), ("sum", f32)], [pltpu.VMEM((40, 16, 128), f32)])
    sums = jnp.sum(total_all(small, n_dp, 5), axis=1)
    g_mix_in, g_mix_res, g_depth = small_grads(sums, mix_in, mix_res, depth)
    g_ff_out = dot(hidden, dbf, ((0,), (0,)))
    g_ff_proj = g_wf.reshape(n_all, rows, 2, ffl).transpose(1, 2, 0, 3).reshape(ff_proj.shape).astype(f32)
    return out, g_in, g_att_proj, g_attn_out, g_ff_proj, g_ff_out, g_mix_in, g_mix_res, g_depth


def solution(mesh):
    n_dp, n_seq = mesh.shape["dp"], mesh.shape["seq"]
    tok = P("dp", "seq", None, None)
    ids = P("dp", "seq")
    mat = P(("dp", "seq"), None)

    body = fast_body if (n_dp, n_seq) == (4, 8) else plain_body

    def run(*args):
        return body(n_dp, n_seq, *args)

    return jax.shard_map(
        run, mesh=mesh,
        in_specs=(tok, ids, ids, mat, mat, mat, mat, P(), P(), P(), tok),
        out_specs=(tok, tok, mat, mat, mat, mat, P(), P(), P()),
        check_vma=False)
```
